256 devices in a mesh: gx: 8 (over z_hi, core), gy: 8 (over z_lo, y), gz: 4 (over x).
Axes of the slice: x: 4, y: 4, z: 8 (z_hi: 4, z_lo: 2; z = z_hi * 2 + z_lo), core: 2. Of those that a mesh axis runs over, the one named last changes fastest.
Arguments:
- blocks: bfloat16 [16, 8, 8, 27, 128, 128], P('gx', 'gy', 'gz')
- pattern: int32 [16, 8, 8, 27], P('gx', 'gy'), may hold values 0 or 1
- order: int32 [16, 8, 8], P('gx', 'gy'), may hold values from 0 to 7, each once within a row
- start: float32 [16, 8, 8, 128], P('gx', 'gy', 'gz'), may hold values from -6 to 6
- rhs: float32 [16, 8, 8, 128], P('gx', 'gy', 'gz'), may hold values from -6 to 6
Outputs:
- smoothed: float32 [16, 8, 8, 128], P('gx', 'gy', 'gz')
- remainder: float32 [16, 8, 8, 128], P('gx', 'gy', 'gz')
The draws below stay inside these ranges and needn't reach their ends.
Inputs may be any that keep to these rules, and one draw needn't show every extreme that they name: `order`: in every grid column the 8 slots name each plane exactly once. `pattern`: entry 13 is ignored.
All inputs are finite; a program needn't handle non-finite values. No bound on the sum of `pattern` on one device may be relied on, other than what follows from the above.
Results may differ from the reference program's by a relative error of at most 0.0081.
Values may be sent and summed in bfloat16 or wider, within the bound.
A program may use at most 64 MiB of HBM per device.

```python
import jax
import jax.numpy as jnp
from jax import lax

BS = 128
STENCIL = 27
DEG = 4
NX = 16
NY = 8
NZ = 8


def draw_blocks(key, part):
    shape = (NX, NY, NZ, STENCIL, BS, BS)
    spread = 0.7 / (STENCIL * BS) ** 0.5
    values = jax.random.normal(key, shape, jnp.float32) * spread
    values = values.at[:, :, :, 13].add(jnp.eye(BS, dtype=jnp.float32))
    return values.astype(jnp.bfloat16)


def place_ends(values, rng, smallest, largest):
    spot = [jax.random.randint(jax.random.fold_in(rng, axis), (), 0, length) for axis, length in enumerate(values.shape)]
    widest = values.shape.index(max(values.shape))
    next_to = spot[:widest] + [(spot[widest] + 1) % values.shape[widest]] + spot[widest + 1:]
    return values.at[tuple(spot)].set(smallest).at[tuple(next_to)].set(largest)


def steps_of(key, shape, split, least, largest):
    level = 1.0
    for dim, shards_of in split:
        heights = jax.random.uniform(jax.random.fold_in(jax.random.fold_in(key, 6), dim), (shards_of,), jnp.float32, least / len(split), largest / len(split))
        level = level * jnp.repeat(jnp.exp(heights), shape[dim] // shards_of).reshape((-1,) + (1,) * (len(shape) - 1 - dim))
    return level


def noise(stream_key, shape, scale, reach, shards=(), held_as=jnp.bfloat16):
    values = scale * jax.random.normal(stream_key, shape, jnp.float32)
    if shards:
        values = values * steps_of(stream_key, shape, shards, -0.22, 0.18)
    return jnp.clip(values, -reach, reach).astype(held_as)


def setup_inputs(seed: int = 0) -> dict:
    arg_keys = jax.random.split(jax.random.key(seed), 6)
    blocks = draw_blocks(jax.random.fold_in(arg_keys[5], 71), 0)
    pattern = place_ends((jax.random.randint(arg_keys[1], (NX, NY, NZ, STENCIL), 0, 4) < 3).astype(jnp.int32), jax.random.fold_in(arg_keys[1], 1), 0, 1)
    order = jax.vmap(lambda own: jax.random.permutation(own, NZ))(jax.random.split(arg_keys[2], NX * NY)).reshape((NX, NY, NZ)).astype(jnp.int32)
    start = noise(arg_keys[3], (NX, NY, NZ, BS), 1.0, 6.0, ((0, 8), (1, 8), (2, 4)), jnp.float32)
    rhs = noise(arg_keys[4], (NX, NY, NZ, BS), 1.0, 6.0, ((0, 8), (1, 8), (2, 4)), jnp.float32)
    return dict(blocks=blocks, pattern=pattern, order=order, start=start, rhs=rhs)


def coupled_values(vector, order, pattern):
    inverse = jnp.argsort(order, axis=2).astype(jnp.int32)
    rounded = vector.astype(jnp.bfloat16).astype(jnp.float32)
    planes = jnp.take_along_axis(rounded, jnp.broadcast_to(inverse[..., None], rounded.shape), axis=2)
    padded = jnp.pad(planes, ((1, 1), (1, 1), (1, 1), (0, 0)))
    span_x, span_y, span_z, width = vector.shape
    pieces = []
    for step_a in range(3):
        for step_b in range(3):
            column = padded[step_a:step_a + span_x, step_b:step_b + span_y]
            for step_c in range(3):
                index = jnp.broadcast_to((order + step_c)[..., None], (span_x, span_y, span_z, width)).astype(jnp.int32)
                pieces.append(jnp.take_along_axis(column, index, axis=2))
    gathered = jnp.stack(pieces, axis=3)
    present = jnp.where(jnp.arange(27) == 13, 1, pattern).astype(jnp.float32)
    return gathered * present[..., None]


def apply_operator(blocks, vector, order, pattern):
    gathered = coupled_values(vector, order, pattern)

    def one_plane(pair):
        values, matrix = pair
        return jnp.einsum("ysoj,ysoij->ysi", values, matrix.astype(jnp.float32))

    return lax.map(one_plane, (gathered, blocks))


def reference(blocks, pattern, order, start, rhs):
    center = 1.0
    spread = 0.8
    sigma = center / spread
    rho = 1.0 / sigma
    smoothed = start
    remainder = rhs - apply_operator(blocks, smoothed, order, pattern)
    search = remainder / center
    for number in range(DEG):
        smoothed = smoothed + search
        remainder = remainder - apply_operator(blocks, search, order, pattern)
        if number + 1 < DEG:
            following = 1.0 / (2.0 * sigma - rho)
            search = following * rho * search + (2.0 * following / spread) * remainder
            rho = following
    return smoothed, remainder
```

```python
import jax
import jax.numpy as jnp
from jax import lax
from jax.experimental import pallas as pl
from jax.experimental.pallas import tpu as pltpu
from jax.sharding import PartitionSpec as P

DEG = 4
MESH = pl.DeviceIdType.MESH

SIDES = (-1, 1, 0)
OFFSETS = [(dx, dy, dz) for dx in SIDES for dy in SIDES for dz in (1, 2, 3, 0)]
PEERS = len(OFFSETS) - 1
HALO = [(dx, dy) for dx in SIDES for dy in SIDES]


def coefficients():
    center, spread = 1.0, 0.8
    sigma = center / spread
    rho = 1.0 / sigma
    old, new = [0.0], [1.0 / center]
    for _ in range(DEG - 1):
        following = 1.0 / (2.0 * sigma - rho)
        old.append(following * rho)
        new.append(2.0 * following / spread)
        rho = following
    return old, new


def kernel(sizes, blocks_hbm, order_ref, pattern_ref, start_ref, rhs_ref, smoothed_ref, remainder_ref,
           blocks, recv, sent, tags, tag_out, select, block_sem, send_sem, recv_sem, tag_send, tag_recv):
    nx, ny, nz = sizes
    gx, gy, gz = (lax.axis_index(a) for a in ("gx", "gy", "gz"))
    wide, _, depth, width = start_ref.shape
    rows = wide * depth
    load = pltpu.make_async_copy(blocks_hbm, blocks, block_sem)
    load.start()

    def at(offset):
        dx, dy, dz = offset
        return (lax.rem(gx + (dx + nx), nx), lax.rem(gy + (dy + ny), ny), lax.rem(gz + dz, nz))

    barrier = pltpu.get_barrier_semaphore()
    for offset in OFFSETS[:PEERS]:
        pl.semaphore_signal(barrier, inc=1, device_id=at(offset), device_id_type=MESH)

    lane = lax.broadcasted_iota(jnp.int32, (8, width), 1)
    period = lane & (4 * rows - 1)
    turn = period // rows
    row = period & (rows - 1)
    below = (gz + 3 - turn) & (nz - 1)
    place = (row // depth) * 8 + below * depth + (row & (depth - 1))
    tag = jnp.zeros((8, width), jnp.float32)
    for column in range(wide):
        for slot in range(8):
            value = order_ref[column, 0, slot].astype(jnp.float32)
            tag = jnp.where(place == column * 8 + slot, value, tag)
    tag_out[...] = tag
    tags[len(HALO) - 1] = tag

    v = start_ref[...].reshape(rows, width)
    sent[0] = v.astype(jnp.bfloat16)
    pl.semaphore_wait(barrier, PEERS)

    for number, (dx, dy) in enumerate(HALO[:-1]):
        pltpu.make_async_remote_copy(
            tag_out, tags.at[number], tag_send, tag_recv, device_id=at((dx, dy, 0)), device_id_type=MESH
        ).start()

    span = 2 * width
    col = lax.broadcasted_iota(jnp.int32, (8, span), 1)
    own = lax.broadcasted_iota(jnp.int32, (8, span), 0)
    halo = col // (4 * rows)
    side_x = (halo >= 3).astype(jnp.int32) + (halo >= 6).astype(jnp.int32)
    side_y = halo - 3 * side_x
    from_x = jnp.where(side_x == 0, 1, jnp.where(side_x == 1, -1, 0))
    from_y = jnp.where(side_y == 0, 1, jnp.where(side_y == 1, -1, 0))
    inside = (
        (gx + from_x >= 0) & (gx + from_x < nx) & (gy + from_y >= 0) & (gy + from_y < ny)
        & (col < 4 * rows * len(HALO)) & (own < rows)
    )
    step_x = wide * from_x + ((col & (rows - 1)) // depth) - (own // depth)
    flat = jnp.where(inside, (step_x + 1) * 3 + from_y + 1, -1)
    flat = jnp.where((step_x < -1) | (step_x > 1), -1, flat)

    sub = lax.broadcasted_iota(jnp.int32, (8, 1), 0)
    mine = jnp.full((8, 1), -100.0, jnp.float32)
    height = lax.broadcasted_iota(jnp.int32, (8, pattern_ref.shape[-1]), 0)
    keep = jnp.zeros((8, pattern_ref.shape[-1]), jnp.int32)
    for column in range(wide):
        present = pattern_ref[column, 0]
        for slot in range(depth):
            r = column * depth + slot
            mine = jnp.where(sub == r, order_ref[column, 0, gz * depth + slot].astype(jnp.float32), mine)
            line = jnp.sum(jnp.where(height == gz * depth + slot, present, 0), axis=0, keepdims=True)
            keep = jnp.where(height == r, line, keep)

    old, new = coefficients()

    def turn_of(number, carry, first=False):
        v, smoothed, remainder = carry
        if not first:
            sent[number] = v.astype(jnp.bfloat16)
        for k, offset in enumerate(OFFSETS[:PEERS]):
            pltpu.make_async_remote_copy(
                sent.at[number], recv.at[number, pl.ds(k * rows, rows)], send_sem.at[number], recv_sem.at[number],
                device_id=at(offset), device_id_type=MESH,
            ).start()
        recv[number, pl.ds(PEERS * rows, rows)] = sent[number]
        if first:
            pltpu.make_async_copy(tags.at[pl.ds(0, len(HALO) - 1)], tags.at[pl.ds(0, len(HALO) - 1)], tag_recv).wait()
            half = lax.broadcasted_iota(jnp.int32, (8, width), 1) // (4 * rows)
            low = jnp.zeros((8, width), jnp.float32)
            for g in range(8):
                low = jnp.where(half == g, tags[g], low)
            plane = jnp.concatenate([low, tags[8]], axis=1)
            level = [plane == mine + float(c - 1) for c in range(3)]
            for o in range(27):
                chosen = (flat == o // 3) & level[o % 3]
                if o != 13:
                    chosen = chosen & (keep[:, o : o + 1] > 0)
                select[pl.ds(8 * o, 8), :] = jnp.where(chosen, 1.0, 0.0)
            load.wait()
        everything = recv.at[number, pl.ds(0, PEERS * rows)]
        pltpu.make_async_copy(everything, everything, recv_sem.at[number]).wait()
        table = select[:, 0 : 4 * rows * len(HALO)].astype(jnp.bfloat16)
        picked = jnp.dot(table, recv[number], preferred_element_type=jnp.float32).astype(jnp.bfloat16)
        pieces = []
        for r in range(rows):
            total = jnp.zeros((8, width), jnp.float32)
            for o in range(27):
                total += lax.dot_general(
                    picked[8 * o : 8 * o + 8], blocks[r * 27 + o], (((1,), (1,)), ((), ())),
                    preferred_element_type=jnp.float32,
                )
            pieces.append(total[r : r + 1])
        product = jnp.concatenate(pieces, axis=0)
        remainder = remainder - product
        smoothed = smoothed + v
        a, b = jnp.float32(old[0]), jnp.float32(new[0])
        for i in range(1, DEG):
            a = jnp.where(number == i, jnp.float32(old[i]), a)
            b = jnp.where(number == i, jnp.float32(new[i]), b)
        return (a * v + b * remainder, smoothed, remainder)

    carry = (v, jnp.zeros_like(v), rhs_ref[...].reshape(rows, width))
    carry = turn_of(0, carry, True)
    _, smoothed, remainder = lax.fori_loop(1, DEG + 1, turn_of, carry)
    smoothed_ref[...] = smoothed.reshape(smoothed_ref.shape)
    remainder_ref[...] = remainder.reshape(remainder_ref.shape)

    others = tags.at[pl.ds(0, len(HALO) - 1)]
    pltpu.make_async_copy(others, others, tag_send).wait()
    for number in range(DEG + 1):
        everything = recv.at[number, pl.ds(0, PEERS * rows)]
        pltpu.make_async_copy(everything, everything, send_sem.at[number]).wait()


def local(sizes, blocks, pattern, order, start, rhs):
    wide, _, depth, width = start.shape
    rows = wide * depth
    flat = blocks.reshape((rows * blocks.shape[3],) + blocks.shape[4:])
    vmem = pl.BlockSpec(memory_space=pltpu.VMEM)
    import functools

    return pl.pallas_call(
        functools.partial(kernel, sizes),
        out_shape=(jax.ShapeDtypeStruct(start.shape, jnp.float32),) * 2,
        in_specs=[
            pl.BlockSpec(memory_space=pl.ANY),
            pl.BlockSpec(memory_space=pltpu.SMEM),
            vmem, vmem, vmem,
        ],
        out_specs=(vmem, vmem),
        scratch_shapes=[
            pltpu.VMEM(flat.shape, jnp.bfloat16),
            pltpu.VMEM((DEG + 1, len(OFFSETS) * rows, width), jnp.bfloat16),
            pltpu.VMEM((DEG + 1, rows, width), jnp.bfloat16),
            pltpu.VMEM((len(HALO), 8, width), jnp.float32),
            pltpu.VMEM((8, width), jnp.float32),
            pltpu.VMEM((8 * 27, 2 * width), jnp.float32),
            pltpu.SemaphoreType.DMA,
            pltpu.SemaphoreType.DMA((DEG + 1,)),
            pltpu.SemaphoreType.DMA((DEG + 1,)),
            pltpu.SemaphoreType.DMA,
            pltpu.SemaphoreType.DMA,
        ],
        compiler_params=pltpu.CompilerParams(collective_id=0, has_side_effects=True),
    )(flat, order, pattern, start, rhs)


def solution(mesh):
    import functools

    in_specs = (
        P("gx", "gy", "gz", None, None, None),
        P("gx", "gy", None, None),
        P("gx", "gy", None),
        P("gx", "gy", "gz", None),
        P("gx", "gy", "gz", None),
    )
    out_specs = (P("gx", "gy", "gz", None), P("gx", "gy", "gz", None))
    sizes = tuple(mesh.shape[a] for a in ("gx", "gy", "gz"))
    return jax.shard_map(
        functools.partial(local, sizes), mesh=mesh, in_specs=in_specs, out_specs=out_specs, check_vma=False
    )
```

```python
import functools

import jax
import jax.numpy as jnp
from jax import lax
from jax.experimental import pallas as pl
from jax.experimental.pallas import tpu as pltpu
from jax.sharding import PartitionSpec as P

DEG = 4
MESH = pl.DeviceIdType.MESH

NEAR = ((-1, 0), (1, 0), (0, -1), (0, 1), (0, 0))
FAR = ((1, 1), (-1, -1), (1, -1), (-1, 1))
TURNS = (1, 2, 3, 0)
ISSUE = (2, 1, 3, 0)
NEAR_ENTRIES = [(9 * a + 3 * b + c, 9 * d + 3 * b + c) for a, d in ((1, 1), (2, 0)) for b in range(3) for c in range(3)]
NEAR_ENTRIES += [(3 + c, 21 + c) for c in range(3)]
FAR_ENTRIES = [(3 * b + c, 18 + 3 * b + c) for b in (0, 2) for c in range(3)]


def coefficients():
    center, spread = 1.0, 0.8
    sigma = center / spread
    rho = 1.0 / sigma
    old, new = [0.0], [1.0 / center]
    for _ in range(DEG - 1):
        following = 1.0 / (2.0 * sigma - rho)
        old.append(following * rho)
        new.append(2.0 * following / spread)
        rho = following
    return old, new


def kernel(sizes, blocks_hbm, order_ref, pattern_hbm, start_hbm, rhs_hbm, out_ref,
           blocks, pattern, first, rhs, near, far, sent, tags, tag_out, near_table, far_table, masks,
           load_sem, send_sem, near_sem, far_sem, tag_send, tag_recv):
    nx, ny, nz = sizes
    gx, gy, gz = (lax.axis_index(a) for a in ("gx", "gy", "gz"))
    wide, _, depth, width = first.shape
    rows = wide * depth
    near_peers, far_peers = 4 * len(NEAR) - 1, 4 * len(FAR)

    def at(dx, dy, dz):
        return (lax.rem(gx + (dx + nx), nx), lax.rem(gy + (dy + ny), ny), lax.rem(gz + dz, nz))

    barrier = pltpu.get_barrier_semaphore()
    for dz in ISSUE:
        for dx, dy in FAR + NEAR:
            if (dx, dy, dz) != (0, 0, 0):
                pl.semaphore_signal(barrier, inc=1, device_id=at(dx, dy, dz), device_id_type=MESH)

    small = [
        pltpu.make_async_copy(a, b, load_sem.at[1 + i])
        for i, (a, b) in enumerate(((start_hbm, first), (rhs_hbm, rhs), (pattern_hbm, pattern)))
    ]
    for copy in small:
        copy.start()
    load = pltpu.make_async_copy(blocks_hbm, blocks, load_sem.at[0])
    load.start()

    lane = lax.broadcasted_iota(jnp.int32, (8, width), 1)
    own = lax.broadcasted_iota(jnp.int32, (8, width), 0)
    period = lane & (4 * rows - 1)
    row = period & (rows - 1)
    below = (gz + 3 - period // rows) & (nz - 1)
    place = (row // depth) * 8 + below * depth + (row & (depth - 1))
    tag = jnp.zeros((8, width), jnp.float32)
    for column in range(wide):
        for slot in range(8):
            value = order_ref[column, 0, slot].astype(jnp.float32)
            tag = jnp.where(place == column * 8 + slot, value, tag)
    tag_out[...] = tag

    for copy in small:
        copy.wait()
    filler = jnp.zeros((8 - rows, width), jnp.float32)
    v = jnp.concatenate([first[...].reshape(rows, width), filler], axis=0)
    remainder = jnp.concatenate([rhs[...].reshape(rows, width), filler], axis=0)
    sent[0] = v[0:rows].astype(jnp.bfloat16)

    def halo(groups):
        group = lane // (4 * rows)
        dx, dy = jnp.zeros_like(lane), jnp.zeros_like(lane)
        for g, (x, y) in enumerate(groups):
            dx = jnp.where(group == g, -x, dx)
            dy = jnp.where(group == g, -y, dy)
        inside = (gx + dx >= 0) & (gx + dx < nx) & (gy + dy >= 0) & (gy + dy < ny)
        inside = inside & (lane < 4 * rows * len(groups)) & (own < rows)
        step = wide * dx + (row // depth) - (own // depth)
        return jnp.where(inside & (step >= -1) & (step <= 1), (step + 1) * 3 + dy + 1, -1)

    mine = jnp.full((8, width), -100.0, jnp.float32)
    height = lax.broadcasted_iota(jnp.int32, (8, pattern.shape[-1]), 0)
    keep = jnp.zeros((8, pattern.shape[-1]), jnp.int32)
    for column in range(wide):
        present = pattern[column, 0]
        for slot in range(depth):
            r = column * depth + slot
            mine = jnp.where(own == r, order_ref[column, 0, gz * depth + slot].astype(jnp.float32), mine)
            line = jnp.sum(jnp.where(height == gz * depth + slot, present, 0), axis=0, keepdims=True)
            keep = jnp.where(height == r, line, keep)

    def premask(entries, groups, base):
        flat = halo(groups)
        for j, (low, high) in enumerate(entries):
            chosen = flat == jnp.where(own < depth, low // 3, high // 3)
            if low != 13:
                held = jnp.where(own[:, 0:1] < depth, keep[:, low : low + 1], keep[:, high : high + 1])
                chosen = chosen & (held > 0)
            masks[base + j] = jnp.where(chosen, 1.0, 0.0)

    premask(NEAR_ENTRIES, NEAR, 0)
    premask(FAR_ENTRIES, FAR, len(NEAR_ENTRIES))

    pl.semaphore_wait(barrier, near_peers + far_peers)

    def send(number):
        for groups, buffer, sem in ((FAR, far, far_sem), (NEAR, near, near_sem)):
            for dz in ISSUE:
                for g, (dx, dy) in enumerate(groups):
                    if (dx, dy, dz) == (0, 0, 0):
                        continue
                    slot = 4 * g + TURNS.index(dz)
                    pltpu.make_async_remote_copy(
                        sent.at[number], buffer.at[number, pl.ds(slot * rows, rows)], send_sem.at[number],
                        sem.at[number], device_id=at(dx, dy, dz), device_id_type=MESH,
                    ).start()

    everyone = FAR + NEAR
    for g, (dx, dy) in enumerate(everyone[:-1]):
        pltpu.make_async_remote_copy(
            tag_out, tags.at[g], tag_send, tag_recv, device_id=at(dx, dy, 0), device_id_type=MESH
        ).start()
    send(0)
    others = tags.at[pl.ds(0, len(everyone) - 1)]
    pltpu.make_async_copy(others, others, tag_recv).wait()
    tags[len(everyone) - 1] = tag

    def finish(entries, base, first_tag, count, table):
        plane = jnp.zeros((8, width), jnp.float32)
        for g in range(count):
            plane = jnp.where(lane // (4 * rows) == g, tags[first_tag + g], plane)
        level = [jnp.where(plane == mine + float(c - 1), 1.0, 0.0) for c in range(3)]
        parts = [masks[base + j] * level[low % 3] for j, (low, _) in enumerate(entries)]
        if len(parts) % 2:
            parts.append(jnp.zeros((8, width), jnp.float32))
        for j in range(0, len(parts), 2):
            both = jnp.concatenate(parts[j : j + 2], axis=0)
            table[pl.ds(8 * j, 16), :] = both.astype(jnp.bfloat16)

    finish(NEAR_ENTRIES, 0, len(FAR), len(NEAR), near_table)
    finish(FAR_ENTRIES, len(NEAR_ENTRIES), 0, len(FAR), far_table)
    load.wait()

    old, new = coefficients()

    def apply(table, count, buffer, entries):
        picked = jnp.dot(table[:, 0:count], buffer, preferred_element_type=jnp.float32)
        left = jnp.concatenate(
            [picked[8 * j : 8 * j + 8].astype(jnp.bfloat16) for j in range(len(entries))], axis=1
        )
        product = jnp.zeros((8, width), jnp.float32)
        for r in range(rows):
            right = jnp.concatenate([blocks[r * 27 + pair[r // depth]] for pair in entries], axis=1)
            total = lax.dot_general(left, right, (((1,), (1,)), ((), ())), preferred_element_type=jnp.float32)
            product = jnp.where(own == r, total, product)
        return product

    def turn_of(number, carry):
        v, smoothed, remainder = carry
        a, b = jnp.float32(old[0]), jnp.float32(new[0])
        for i in range(1, DEG):
            a = jnp.where(number == i, jnp.float32(old[i]), a)
            b = jnp.where(number == i, jnp.float32(new[i]), b)
        near[number, pl.ds(near_peers * rows, rows)] = sent[number]
        theirs = near.at[number, pl.ds(0, near_peers * rows)]
        pltpu.make_async_copy(theirs, theirs, near_sem.at[number]).wait()
        partial = remainder - apply(near_table, 4 * rows * len(NEAR), near[number], NEAR_ENTRIES)
        theirs = far.at[number]
        pltpu.make_async_copy(theirs, theirs, far_sem.at[number]).wait()
        remainder = partial - apply(far_table, 4 * rows * len(FAR), far[number], FAR_ENTRIES)
        following = a * v + b * remainder

        @pl.when(number < DEG)
        def _():
            sent[number + 1] = following[0:rows].astype(jnp.bfloat16)
            send(number + 1)

        return following, smoothed + v, remainder

    _, smoothed, remainder = lax.fori_loop(0, DEG + 1, turn_of, (v, jnp.zeros_like(v), remainder))
    out_ref[0] = smoothed[0:rows].reshape(first.shape)
    out_ref[1] = remainder[0:rows].reshape(first.shape)

    pltpu.make_async_copy(others, others, tag_send).wait()

    def drain(number, carry):
        theirs = near.at[number, pl.ds(0, near_peers * rows)]
        pltpu.make_async_copy(theirs, theirs, send_sem.at[number]).wait()
        theirs = far.at[number]
        pltpu.make_async_copy(theirs, theirs, send_sem.at[number]).wait()
        return carry

    lax.fori_loop(0, DEG + 1, drain, 0)


def split(both_ref, smoothed_ref, remainder_ref):
    smoothed_ref[...] = both_ref[0]
    remainder_ref[...] = both_ref[1]


def local(sizes, blocks, pattern, order, start, rhs):
    wide, _, depth, width = start.shape
    rows = wide * depth
    flat = blocks.reshape((rows * blocks.shape[3],) + blocks.shape[4:])
    vmem = pl.BlockSpec(memory_space=pltpu.VMEM)
    anywhere = pl.BlockSpec(memory_space=pl.ANY)
    near_blocks, far_blocks = (len(NEAR_ENTRIES) + 1) // 2, (len(FAR_ENTRIES) + 1) // 2
    both = pl.pallas_call(
        functools.partial(kernel, sizes),
        out_shape=jax.ShapeDtypeStruct((2,) + start.shape, jnp.float32),
        in_specs=[anywhere, pl.BlockSpec(memory_space=pltpu.SMEM), anywhere, anywhere, anywhere],
        out_specs=vmem,
        scratch_shapes=[
            pltpu.VMEM(flat.shape, jnp.bfloat16),
            pltpu.VMEM(pattern.shape, jnp.int32),
            pltpu.VMEM(start.shape, jnp.float32),
            pltpu.VMEM(start.shape, jnp.float32),
            pltpu.VMEM((DEG + 1, 4 * rows * len(NEAR), width), jnp.bfloat16),
            pltpu.VMEM((DEG + 1, 4 * rows * len(FAR), width), jnp.bfloat16),
            pltpu.VMEM((DEG + 1, rows, width), jnp.bfloat16),
            pltpu.VMEM((len(NEAR) + len(FAR), 8, width), jnp.float32),
            pltpu.VMEM((8, width), jnp.float32),
            pltpu.VMEM((16 * near_blocks, width), jnp.bfloat16),
            pltpu.VMEM((16 * far_blocks, width), jnp.bfloat16),
            pltpu.VMEM((len(NEAR_ENTRIES) + len(FAR_ENTRIES), 8, width), jnp.float32),
            pltpu.SemaphoreType.DMA((4,)),
            pltpu.SemaphoreType.DMA((DEG + 1,)),
            pltpu.SemaphoreType.DMA((DEG + 1,)),
            pltpu.SemaphoreType.DMA((DEG + 1,)),
            pltpu.SemaphoreType.DMA,
            pltpu.SemaphoreType.DMA,
        ],
        compiler_params=pltpu.CompilerParams(collective_id=0, has_side_effects=True),
    )(flat, order, pattern, start, rhs)
    piece = jax.ShapeDtypeStruct(start.shape, jnp.float32)
    return pl.pallas_call(split, out_shape=(piece, piece), in_specs=[vmem], out_specs=(vmem, vmem))(both)


def solution(mesh):
    in_specs = (
        P("gx", "gy", "gz", None, None, None),
        P("gx", "gy", None, None),
        P("gx", "gy", None),
        P("gx", "gy", "gz", None),
        P("gx", "gy", "gz", None),
    )
    out_specs = (P("gx", "gy", "gz", None), P("gx", "gy", "gz", None))
    sizes = tuple(mesh.shape[a] for a in ("gx", "gy", "gz"))
    return jax.shard_map(
        functools.partial(local, sizes), mesh=mesh, in_specs=in_specs, out_specs=out_specs, check_vma=False
    )
```

```python
import functools

import jax
import jax.numpy as jnp
from jax import lax
from jax.experimental import pallas as pl
from jax.experimental.pallas import tpu as pltpu
from jax.sharding import PartitionSpec as P

DEG = 4
MESH = pl.DeviceIdType.MESH

NEAR = ((-1, 0), (1, 0), (0, -1), (0, 1), (0, 0))
FAR = ((1, 1), (-1, -1), (1, -1), (-1, 1))
TURNS = (1, 2, 3, 0)
ISSUE = (2, 1, 3, 0)
NEAR_ENTRIES = [(9 * a + 3 * b + c, 9 * d + 3 * b + c) for a, d in ((1, 1), (2, 0)) for b in range(3) for c in range(3)]
NEAR_ENTRIES += [(3 + c, 21 + c) for c in range(3)]
FAR_ENTRIES = [(3 * b + c, 18 + 3 * b + c) for b in (0, 2) for c in range(3)]


def coefficients():
    center, spread = 1.0, 0.8
    sigma = center / spread
    rho = 1.0 / sigma
    old, new = [0.0], [1.0 / center]
    for _ in range(DEG - 1):
        following = 1.0 / (2.0 * sigma - rho)
        old.append(following * rho)
        new.append(2.0 * following / spread)
        rho = following
    return old, new


def kernel(sizes, blocks_hbm, order_hbm, pattern_hbm, start_hbm, rhs_hbm, out_ref,
           blocks, order_ref, pattern, first, rhs, near, far, sent, tags, tag_out, near_table, far_table, masks,
           load_sem, send_sem, near_sem, far_sem, tag_send, tag_recv):
    nx, ny, nz = sizes
    gx, gy, gz = (lax.axis_index(a) for a in ("gx", "gy", "gz"))
    wide, _, depth, width = first.shape
    rows = wide * depth
    near_peers, far_peers = 4 * len(NEAR) - 1, 4 * len(FAR)

    def at(dx, dy, dz):
        return (lax.rem(gx + (dx + nx), nx), lax.rem(gy + (dy + ny), ny), lax.rem(gz + dz, nz))

    barrier = pltpu.get_barrier_semaphore()
    for dz in ISSUE:
        for dx, dy in FAR + NEAR:
            if (dx, dy, dz) != (0, 0, 0):
                pl.semaphore_signal(barrier, inc=1, device_id=at(dx, dy, dz), device_id_type=MESH)

    small = [
        pltpu.make_async_copy(a, b, load_sem.at[1 + i])
        for i, (a, b) in enumerate(((order_hbm, order_ref), (start_hbm, first), (rhs_hbm, rhs), (pattern_hbm, pattern)))
    ]
    for copy in small:
        copy.start()
    load = pltpu.make_async_copy(blocks_hbm, blocks, load_sem.at[0])
    load.start()

    small[0].wait()
    lane = lax.broadcasted_iota(jnp.int32, (8, width), 1)
    own = lax.broadcasted_iota(jnp.int32, (8, width), 0)
    period = lane & (4 * rows - 1)
    row = period & (rows - 1)
    below = (gz + 3 - period // rows) & (nz - 1)
    place = (row // depth) * 8 + below * depth + (row & (depth - 1))
    tag = jnp.zeros((8, width), jnp.float32)
    for column in range(wide):
        for slot in range(8):
            value = order_ref[column, 0, slot].astype(jnp.float32)
            tag = jnp.where(place == column * 8 + slot, value, tag)
    tag_out[...] = tag

    for copy in small[1:]:
        copy.wait()
    filler = jnp.zeros((8 - rows, width), jnp.float32)
    v = jnp.concatenate([first[...].reshape(rows, width), filler], axis=0)
    remainder = jnp.concatenate([rhs[...].reshape(rows, width), filler], axis=0)
    sent[0] = v[0:rows].astype(jnp.bfloat16)

    def halo(groups):
        group = lane // (4 * rows)
        dx, dy = jnp.zeros_like(lane), jnp.zeros_like(lane)
        for g, (x, y) in enumerate(groups):
            dx = jnp.where(group == g, -x, dx)
            dy = jnp.where(group == g, -y, dy)
        inside = (gx + dx >= 0) & (gx + dx < nx) & (gy + dy >= 0) & (gy + dy < ny)
        inside = inside & (lane < 4 * rows * len(groups)) & (own < rows)
        step = wide * dx + (row // depth) - (own // depth)
        return jnp.where(inside & (step >= -1) & (step <= 1), (step + 1) * 3 + dy + 1, -1)

    mine = jnp.full((8, width), -100.0, jnp.float32)
    height = lax.broadcasted_iota(jnp.int32, (8, pattern.shape[-1]), 0)
    keep = jnp.zeros((8, pattern.shape[-1]), jnp.int32)
    for column in range(wide):
        present = pattern[column, 0]
        for slot in range(depth):
            r = column * depth + slot
            mine = jnp.where(own == r, order_ref[column, 0, gz * depth + slot].astype(jnp.float32), mine)
            line = jnp.sum(jnp.where(height == gz * depth + slot, present, 0), axis=0, keepdims=True)
            keep = jnp.where(height == r, line, keep)

    def premask(entries, groups, base):
        flat = halo(groups)
        for j, (low, high) in enumerate(entries):
            chosen = flat == jnp.where(own < depth, low // 3, high // 3)
            if low != 13:
                held = jnp.where(own[:, 0:1] < depth, keep[:, low : low + 1], keep[:, high : high + 1])
                chosen = chosen & (held > 0)
            masks[base + j] = jnp.where(chosen, 1.0, 0.0)

    premask(NEAR_ENTRIES, NEAR, 0)
    premask(FAR_ENTRIES, FAR, len(NEAR_ENTRIES))

    pl.semaphore_wait(barrier, near_peers + far_peers)

    def send(number):
        for groups, buffer, sem in ((FAR, far, far_sem), (NEAR, near, near_sem)):
            for dz in ISSUE:
                for g, (dx, dy) in enumerate(groups):
                    if (dx, dy, dz) == (0, 0, 0):
                        continue
                    slot = 4 * g + TURNS.index(dz)
                    pltpu.make_async_remote_copy(
                        sent.at[number], buffer.at[number, pl.ds(slot * rows, rows)], send_sem.at[number],
                        sem.at[number], device_id=at(dx, dy, dz), device_id_type=MESH,
                    ).start()

    everyone = FAR + NEAR
    for g, (dx, dy) in enumerate(everyone[:-1]):
        pltpu.make_async_remote_copy(
            tag_out, tags.at[g], tag_send, tag_recv, device_id=at(dx, dy, 0), device_id_type=MESH
        ).start()
    send(0)
    others = tags.at[pl.ds(0, len(everyone) - 1)]
    pltpu.make_async_copy(others, others, tag_recv).wait()
    tags[len(everyone) - 1] = tag

    def finish(entries, base, first_tag, count, table):
        plane = jnp.zeros((8, width), jnp.float32)
        for g in range(count):
            plane = jnp.where(lane // (4 * rows) == g, tags[first_tag + g], plane)
        level = [jnp.where(plane == mine + float(c - 1), 1.0, 0.0) for c in range(3)]
        parts = [masks[base + j] * level[low % 3] for j, (low, _) in enumerate(entries)]
        if len(parts) % 2:
            parts.append(jnp.zeros((8, width), jnp.float32))
        for j in range(0, len(parts), 2):
            both = jnp.concatenate(parts[j : j + 2], axis=0)
            table[pl.ds(8 * j, 16), :] = both.astype(jnp.bfloat16)

    finish(NEAR_ENTRIES, 0, len(FAR), len(NEAR), near_table)
    finish(FAR_ENTRIES, len(NEAR_ENTRIES), 0, len(FAR), far_table)
    load.wait()

    old, new = coefficients()

    def apply(table, count, buffer, entries):
        picked = jnp.dot(table[:, 0:count], buffer, preferred_element_type=jnp.float32)
        left = jnp.concatenate(
            [picked[8 * j : 8 * j + 8].astype(jnp.bfloat16) for j in range(len(entries))], axis=1
        )
        product = jnp.zeros((8, width), jnp.float32)
        for r in range(rows):
            right = jnp.concatenate([blocks[r * 27 + pair[r // depth]] for pair in entries], axis=1)
            total = lax.dot_general(left, right, (((1,), (1,)), ((), ())), preferred_element_type=jnp.float32)
            product = jnp.where(own == r, total, product)
        return product

    def turn_of(number, carry):
        v, smoothed, remainder = carry
        a, b = jnp.float32(old[0]), jnp.float32(new[0])
        for i in range(1, DEG):
            a = jnp.where(number == i, jnp.float32(old[i]), a)
            b = jnp.where(number == i, jnp.float32(new[i]), b)
        near[number, pl.ds(near_peers * rows, rows)] = sent[number]
        theirs = near.at[number, pl.ds(0, near_peers * rows)]
        pltpu.make_async_copy(theirs, theirs, near_sem.at[number]).wait()
        partial = remainder - apply(near_table, 4 * rows * len(NEAR), near[number], NEAR_ENTRIES)
        theirs = far.at[number]
        pltpu.make_async_copy(theirs, theirs, far_sem.at[number]).wait()
        remainder = partial - apply(far_table, 4 * rows * len(FAR), far[number], FAR_ENTRIES)
        following = a * v + b * remainder

        @pl.when(number < DEG)
        def _():
            sent[number + 1] = following[0:rows].astype(jnp.bfloat16)
            send(number + 1)

        return following, smoothed + v, remainder

    _, smoothed, remainder = lax.fori_loop(0, DEG + 1, turn_of, (v, jnp.zeros_like(v), remainder))
    out_ref[0] = smoothed[0:rows].reshape(first.shape)
    out_ref[1] = remainder[0:rows].reshape(first.shape)

    pltpu.make_async_copy(others, others, tag_send).wait()

    def drain(number, carry):
        theirs = near.at[number, pl.ds(0, near_peers * rows)]
        pltpu.make_async_copy(theirs, theirs, send_sem.at[number]).wait()
        theirs = far.at[number]
        pltpu.make_async_copy(theirs, theirs, send_sem.at[number]).wait()
        return carry

    lax.fori_loop(0, DEG + 1, drain, 0)


def split(both_ref, smoothed_ref, remainder_ref):
    smoothed_ref[...] = both_ref[0]
    remainder_ref[...] = both_ref[1]


def local(sizes, blocks, pattern, order, start, rhs):
    wide, _, depth, width = start.shape
    rows = wide * depth
    flat = blocks.reshape((rows * blocks.shape[3],) + blocks.shape[4:])
    vmem = pl.BlockSpec(memory_space=pltpu.VMEM)
    anywhere = pl.BlockSpec(memory_space=pl.ANY)
    near_blocks, far_blocks = (len(NEAR_ENTRIES) + 1) // 2, (len(FAR_ENTRIES) + 1) // 2
    both = pl.pallas_call(
        functools.partial(kernel, sizes),
        out_shape=pltpu.VMEM((2,) + start.shape, jnp.float32),
        in_specs=[anywhere, anywhere, anywhere, anywhere, anywhere],
        out_specs=vmem,
        scratch_shapes=[
            pltpu.VMEM(flat.shape, jnp.bfloat16),
            pltpu.SMEM(order.shape, jnp.int32),
            pltpu.VMEM(pattern.shape, jnp.int32),
            pltpu.VMEM(start.shape, jnp.float32),
            pltpu.VMEM(start.shape, jnp.float32),
            pltpu.VMEM((DEG + 1, 4 * rows * len(NEAR), width), jnp.bfloat16),
            pltpu.VMEM((DEG + 1, 4 * rows * len(FAR), width), jnp.bfloat16),
            pltpu.VMEM((DEG + 1, rows, width), jnp.bfloat16),
            pltpu.VMEM((len(NEAR) + len(FAR), 8, width), jnp.float32),
            pltpu.VMEM((8, width), jnp.float32),
            pltpu.VMEM((16 * near_blocks, width), jnp.bfloat16),
            pltpu.VMEM((16 * far_blocks, width), jnp.bfloat16),
            pltpu.VMEM((len(NEAR_ENTRIES) + len(FAR_ENTRIES), 8, width), jnp.float32),
            pltpu.SemaphoreType.DMA((5,)),
            pltpu.SemaphoreType.DMA((DEG + 1,)),
            pltpu.SemaphoreType.DMA((DEG + 1,)),
            pltpu.SemaphoreType.DMA((DEG + 1,)),
            pltpu.SemaphoreType.DMA,
            pltpu.SemaphoreType.DMA,
        ],
        compiler_params=pltpu.CompilerParams(collective_id=0, has_side_effects=True),
    )(flat, order, pattern, start, rhs)
    both = pltpu.with_memory_space_constraint(both, pltpu.VMEM)
    piece = jax.ShapeDtypeStruct(start.shape, jnp.float32)
    return pl.pallas_call(split, out_shape=(piece, piece), in_specs=[vmem], out_specs=(vmem, vmem))(both)


def solution(mesh):
    in_specs = (
        P("gx", "gy", "gz", None, None, None),
        P("gx", "gy", None, None),
        P("gx", "gy", None),
        P("gx", "gy", "gz", None),
        P("gx", "gy", "gz", None),
    )
    out_specs = (P("gx", "gy", "gz", None), P("gx", "gy", "gz", None))
    sizes = tuple(mesh.shape[a] for a in ("gx", "gy", "gz"))
    return jax.shard_map(
        functools.partial(local, sizes), mesh=mesh, in_specs=in_specs, out_specs=out_specs, check_vma=False
    )
```

```python
import functools

import jax
import jax.numpy as jnp
from jax import lax
from jax.experimental import pallas as pl
from jax.experimental.pallas import tpu as pltpu
from jax.sharding import PartitionSpec as P

DEG = 4
MESH = pl.DeviceIdType.MESH

NEAR = ((-1, 0), (1, 0), (0, -1), (0, 1), (0, 0))
FAR = ((1, 1), (-1, -1), (1, -1), (-1, 1))
TURNS = (1, 2, 3, 0)
ISSUE = (2, 1, 3, 0)
NEAR_ENTRIES = [(9 * a + 3 * b + c, 9 * d + 3 * b + c) for a, d in ((1, 1), (2, 0)) for b in range(3) for c in range(3)]
NEAR_ENTRIES += [(3 + c, 21 + c) for c in range(3)]
FAR_ENTRIES = [(3 * b + c, 18 + 3 * b + c) for b in (0, 2) for c in range(3)]


def coefficients():
    center, spread = 1.0, 0.8
    sigma = center / spread
    rho = 1.0 / sigma
    old, new = [0.0], [1.0 / center]
    for _ in range(DEG - 1):
        following = 1.0 / (2.0 * sigma - rho)
        old.append(following * rho)
        new.append(2.0 * following / spread)
        rho = following
    return old, new


def kernel(sizes, blocks_hbm, order_hbm, pattern_hbm, start_hbm, rhs_hbm, out_ref,
           blocks, turned, order_ref, pattern, first, rhs, near, far, sent, tags, tag_out, near_table, far_table, masks,
           load_sem, send_sem, near_sem, far_sem, tag_send, tag_recv):
    nx, ny, nz = sizes
    gx, gy, gz = (lax.axis_index(a) for a in ("gx", "gy", "gz"))
    wide, _, depth, width = first.shape
    rows = wide * depth
    near_peers, far_peers = 4 * len(NEAR) - 1, 4 * len(FAR)

    def at(dx, dy, dz):
        return (lax.rem(gx + (dx + nx), nx), lax.rem(gy + (dy + ny), ny), lax.rem(gz + dz, nz))

    barrier = pltpu.get_barrier_semaphore()
    for dz in ISSUE:
        for dx, dy in FAR + NEAR:
            if (dx, dy, dz) != (0, 0, 0):
                pl.semaphore_signal(barrier, inc=1, device_id=at(dx, dy, dz), device_id_type=MESH)

    small = [
        pltpu.make_async_copy(a, b, load_sem.at[1 + i])
        for i, (a, b) in enumerate(((order_hbm, order_ref), (start_hbm, first), (rhs_hbm, rhs), (pattern_hbm, pattern)))
    ]
    for copy in small:
        copy.start()
    load = pltpu.make_async_copy(blocks_hbm, blocks, load_sem.at[0])
    load.start()

    small[0].wait()
    lane = lax.broadcasted_iota(jnp.int32, (8, width), 1)
    own = lax.broadcasted_iota(jnp.int32, (8, width), 0)
    period = lane & (4 * rows - 1)
    row = period & (rows - 1)
    below = (gz + 3 - period // rows) & (nz - 1)
    place = (row // depth) * 8 + below * depth + (row & (depth - 1))
    tag = jnp.zeros((8, width), jnp.float32)
    for column in range(wide):
        for slot in range(8):
            value = order_ref[column, 0, slot].astype(jnp.float32)
            tag = jnp.where(place == column * 8 + slot, value, tag)
    tag_out[...] = tag

    for copy in small[1:]:
        copy.wait()
    filler = jnp.zeros((8 - rows, width), jnp.float32)
    v = jnp.concatenate([first[...].reshape(rows, width), filler], axis=0)
    remainder = jnp.concatenate([rhs[...].reshape(rows, width), filler], axis=0)
    sent[0] = v[0:rows].astype(jnp.bfloat16)

    def halo(groups):
        group = lane // (4 * rows)
        dx, dy = jnp.zeros_like(lane), jnp.zeros_like(lane)
        for g, (x, y) in enumerate(groups):
            dx = jnp.where(group == g, -x, dx)
            dy = jnp.where(group == g, -y, dy)
        inside = (gx + dx >= 0) & (gx + dx < nx) & (gy + dy >= 0) & (gy + dy < ny)
        inside = inside & (lane < 4 * rows * len(groups)) & (own < rows)
        step = wide * dx + (row // depth) - (own // depth)
        return jnp.where(inside & (step >= -1) & (step <= 1), (step + 1) * 3 + dy + 1, -1)

    mine = jnp.full((8, width), -100.0, jnp.float32)
    height = lax.broadcasted_iota(jnp.int32, (8, pattern.shape[-1]), 0)
    keep = jnp.zeros((8, pattern.shape[-1]), jnp.int32)
    for column in range(wide):
        present = pattern[column, 0]
        for slot in range(depth):
            r = column * depth + slot
            mine = jnp.where(own == r, order_ref[column, 0, gz * depth + slot].astype(jnp.float32), mine)
            line = jnp.sum(jnp.where(height == gz * depth + slot, present, 0), axis=0, keepdims=True)
            keep = jnp.where(height == r, line, keep)

    def premask(entries, groups, base):
        flat = halo(groups)
        for j, (low, high) in enumerate(entries):
            chosen = flat == jnp.where(own < depth, low // 3, high // 3)
            if low != 13:
                held = jnp.where(own[:, 0:1] < depth, keep[:, low : low + 1], keep[:, high : high + 1])
                chosen = chosen & (held > 0)
            masks[base + j] = jnp.where(chosen, 1.0, 0.0)

    premask(NEAR_ENTRIES, NEAR, 0)
    premask(FAR_ENTRIES, FAR, len(NEAR_ENTRIES))

    pl.semaphore_wait(barrier, near_peers + far_peers)

    def send(number):
        for groups, buffer, sem in ((FAR, far, far_sem), (NEAR, near, near_sem)):
            for dz in ISSUE:
                for g, (dx, dy) in enumerate(groups):
                    if (dx, dy, dz) == (0, 0, 0):
                        continue
                    slot = 4 * g + TURNS.index(dz)
                    pltpu.make_async_remote_copy(
                        sent.at[number], buffer.at[number, pl.ds(slot * rows, rows)], send_sem.at[number],
                        sem.at[number], device_id=at(dx, dy, dz), device_id_type=MESH,
                    ).start()

    everyone = FAR + NEAR
    for g, (dx, dy) in enumerate(everyone[:-1]):
        pltpu.make_async_remote_copy(
            tag_out, tags.at[g], tag_send, tag_recv, device_id=at(dx, dy, 0), device_id_type=MESH
        ).start()
    send(0)

    load.wait()
    unit = lax.broadcasted_iota(jnp.int32, (width, width), 0) == lax.broadcasted_iota(jnp.int32, (width, width), 1)
    unit = jnp.where(unit, 1.0, 0.0).astype(jnp.bfloat16)

    def turn_block(step, carry):
        for k in range(6):
            block = blocks[6 * step + k]
            flipped = block.T
            turned[6 * step + k] = flipped.astype(jnp.bfloat16)
        return carry

    lax.fori_loop(0, rows * 27 // 6, turn_block, 0)
    others = tags.at[pl.ds(0, len(everyone) - 1)]
    pltpu.make_async_copy(others, others, tag_recv).wait()
    tags[len(everyone) - 1] = tag

    def finish(entries, base, first_tag, count, table):
        plane = jnp.zeros((8, width), jnp.float32)
        for g in range(count):
            plane = jnp.where(lane // (4 * rows) == g, tags[first_tag + g], plane)
        level = [jnp.where(plane == mine + float(c - 1), 1.0, 0.0) for c in range(3)]
        parts = [masks[base + j] * level[low % 3] for j, (low, _) in enumerate(entries)]
        if len(parts) % 2:
            parts.append(jnp.zeros((8, width), jnp.float32))
        for j in range(0, len(parts), 2):
            both = jnp.concatenate(parts[j : j + 2], axis=0)
            table[pl.ds(8 * j, 16), :] = both.astype(jnp.bfloat16)

    finish(NEAR_ENTRIES, 0, len(FAR), len(NEAR), near_table)
    finish(FAR_ENTRIES, len(NEAR_ENTRIES), 0, len(FAR), far_table)

    old, new = coefficients()

    def apply(table, count, buffer, entries):
        picked = jnp.dot(table[:, 0:count], buffer, preferred_element_type=jnp.float32)
        left = jnp.concatenate(
            [picked[8 * j : 8 * j + 8].astype(jnp.bfloat16) for j in range(len(entries))], axis=1
        )
        product = jnp.zeros((8, width), jnp.float32)
        for r in range(0, rows, depth):
            right = jnp.concatenate(
                [
                    jnp.concatenate([turned[(r + s) * 27 + pair[r // depth]] for s in range(depth)], axis=1)
                    for pair in entries
                ],
                axis=0,
            )
            total = jnp.dot(left, right, preferred_element_type=jnp.float32)
            for s in range(depth):
                product = jnp.where(own == r + s, total[:, s * width : (s + 1) * width], product)
        return product

    def turn_of(number, carry):
        v, smoothed, remainder = carry
        a, b = jnp.float32(old[0]), jnp.float32(new[0])
        for i in range(1, DEG):
            a = jnp.where(number == i, jnp.float32(old[i]), a)
            b = jnp.where(number == i, jnp.float32(new[i]), b)
        near[number, pl.ds(near_peers * rows, rows)] = sent[number]
        theirs = near.at[number, pl.ds(0, near_peers * rows)]
        pltpu.make_async_copy(theirs, theirs, near_sem.at[number]).wait()
        partial = remainder - apply(near_table, 4 * rows * len(NEAR), near[number], NEAR_ENTRIES)
        theirs = far.at[number]
        pltpu.make_async_copy(theirs, theirs, far_sem.at[number]).wait()
        remainder = partial - apply(far_table, 4 * rows * len(FAR), far[number], FAR_ENTRIES)
        following = a * v + b * remainder

        @pl.when(number < DEG)
        def _():
            sent[number + 1] = following[0:rows].astype(jnp.bfloat16)
            send(number + 1)

        return following, smoothed + v, remainder

    _, smoothed, remainder = lax.fori_loop(0, DEG + 1, turn_of, (v, jnp.zeros_like(v), remainder))
    out_ref[0] = smoothed[0:rows].reshape(first.shape)
    out_ref[1] = remainder[0:rows].reshape(first.shape)

    pltpu.make_async_copy(others, others, tag_send).wait()

    def drain(number, carry):
        theirs = near.at[number, pl.ds(0, near_peers * rows)]
        pltpu.make_async_copy(theirs, theirs, send_sem.at[number]).wait()
        theirs = far.at[number]
        pltpu.make_async_copy(theirs, theirs, send_sem.at[number]).wait()
        return carry

    lax.fori_loop(0, DEG + 1, drain, 0)


def split(both_ref, smoothed_ref, remainder_ref):
    smoothed_ref[...] = both_ref[0]
    remainder_ref[...] = both_ref[1]


def local(sizes, blocks, pattern, order, start, rhs):
    wide, _, depth, width = start.shape
    rows = wide * depth
    flat = blocks.reshape((rows * blocks.shape[3],) + blocks.shape[4:])
    vmem = pl.BlockSpec(memory_space=pltpu.VMEM)
    anywhere = pl.BlockSpec(memory_space=pl.ANY)
    near_blocks, far_blocks = (len(NEAR_ENTRIES) + 1) // 2, (len(FAR_ENTRIES) + 1) // 2
    both = pl.pallas_call(
        functools.partial(kernel, sizes),
        out_shape=pltpu.VMEM((2,) + start.shape, jnp.float32),
        in_specs=[anywhere, anywhere, anywhere, anywhere, anywhere],
        out_specs=vmem,
        scratch_shapes=[
            pltpu.VMEM(flat.shape, jnp.bfloat16),
            pltpu.VMEM(flat.shape, jnp.bfloat16),
            pltpu.SMEM(order.shape, jnp.int32),
            pltpu.VMEM(pattern.shape, jnp.int32),
            pltpu.VMEM(start.shape, jnp.float32),
            pltpu.VMEM(start.shape, jnp.float32),
            pltpu.VMEM((DEG + 1, 4 * rows * len(NEAR), width), jnp.bfloat16),
            pltpu.VMEM((DEG + 1, 4 * rows * len(FAR), width), jnp.bfloat16),
            pltpu.VMEM((DEG + 1, rows, width), jnp.bfloat16),
            pltpu.VMEM((len(NEAR) + len(FAR), 8, width), jnp.float32),
            pltpu.VMEM((8, width), jnp.float32),
            pltpu.VMEM((16 * near_blocks, width), jnp.bfloat16),
            pltpu.VMEM((16 * far_blocks, width), jnp.bfloat16),
            pltpu.VMEM((len(NEAR_ENTRIES) + len(FAR_ENTRIES), 8, width), jnp.float32),
            pltpu.SemaphoreType.DMA((5,)),
            pltpu.SemaphoreType.DMA((DEG + 1,)),
            pltpu.SemaphoreType.DMA((DEG + 1,)),
            pltpu.SemaphoreType.DMA((DEG + 1,)),
            pltpu.SemaphoreType.DMA,
            pltpu.SemaphoreType.DMA,
        ],
        compiler_params=pltpu.CompilerParams(collective_id=0, has_side_effects=True),
    )(flat, order, pattern, start, rhs)
    both = pltpu.with_memory_space_constraint(both, pltpu.VMEM)
    piece = jax.ShapeDtypeStruct(start.shape, jnp.float32)
    return pl.pallas_call(split, out_shape=(piece, piece), in_specs=[vmem], out_specs=(vmem, vmem))(both)


def solution(mesh):
    in_specs = (
        P("gx", "gy", "gz", None, None, None),
        P("gx", "gy", None, None),
        P("gx", "gy", None),
        P("gx", "gy", "gz", None),
        P("gx", "gy", "gz", None),
    )
    out_specs = (P("gx", "gy", "gz", None), P("gx", "gy", "gz", None))
    sizes = tuple(mesh.shape[a] for a in ("gx", "gy", "gz"))
    return jax.shard_map(
        functools.partial(local, sizes), mesh=mesh, in_specs=in_specs, out_specs=out_specs, check_vma=False
    )
```

```python
import functools

import jax
import jax.numpy as jnp
from jax import lax
from jax.experimental import pallas as pl
from jax.experimental.pallas import tpu as pltpu
from jax.sharding import PartitionSpec as P

DEG = 4
MESH = pl.DeviceIdType.MESH

NEAR = ((-1, 0), (1, 0), (0, -1), (0, 1), (0, 0))
FAR = ((1, 1), (-1, -1), (1, -1), (-1, 1))
TURNS = (1, 2, 3, 0)
ISSUE = (2, 1, 3, 0)
NEAR_ENTRIES = [(9 * a + 3 * b + c, 9 * d + 3 * b + c) for a, d in ((1, 1), (2, 0)) for b in range(3) for c in range(3)]
NEAR_ENTRIES += [(3 + c, 21 + c) for c in range(3)]
FAR_ENTRIES = [(3 * b + c, 18 + 3 * b + c) for b in (0, 2) for c in range(3)]


def coefficients():
    center, spread = 1.0, 0.8
    sigma = center / spread
    rho = 1.0 / sigma
    old, new = [0.0], [1.0 / center]
    for _ in range(DEG - 1):
        following = 1.0 / (2.0 * sigma - rho)
        old.append(following * rho)
        new.append(2.0 * following / spread)
        rho = following
    return old, new


def kernel(sizes, blocks_hbm, order_hbm, pattern_hbm, start_hbm, rhs_hbm, out_ref,
           blocks, turned, order_ref, pattern, first, rhs, near, far, sent, tags, tag_out, near_table, masks, far_rows, spots, spot_of,
           load_sem, send_sem, near_sem, far_sem, tag_send, tag_recv):
    nx, ny, nz = sizes
    gx, gy, gz = (lax.axis_index(a) for a in ("gx", "gy", "gz"))
    wide, _, depth, width = first.shape
    rows = wide * depth
    near_peers, far_peers = 4 * len(NEAR) - 1, 4 * len(FAR)

    def at(dx, dy, dz):
        return (lax.rem(gx + (dx + nx), nx), lax.rem(gy + (dy + ny), ny), lax.rem(gz + dz, nz))

    barrier = pltpu.get_barrier_semaphore()
    for dz in ISSUE:
        for dx, dy in FAR + NEAR:
            if (dx, dy, dz) != (0, 0, 0):
                pl.semaphore_signal(barrier, inc=1, device_id=at(dx, dy, dz), device_id_type=MESH)

    small = [
        pltpu.make_async_copy(a, b, load_sem.at[1 + i])
        for i, (a, b) in enumerate(((order_hbm, order_ref), (start_hbm, first), (rhs_hbm, rhs), (pattern_hbm, pattern)))
    ]
    for copy in small:
        copy.start()
    load = pltpu.make_async_copy(blocks_hbm, blocks, load_sem.at[0])
    load.start()

    small[0].wait()
    lane = lax.broadcasted_iota(jnp.int32, (8, width), 1)
    own = lax.broadcasted_iota(jnp.int32, (8, width), 0)
    period = lane & (4 * rows - 1)
    row = period & (rows - 1)
    below = (gz + 3 - period // rows) & (nz - 1)
    place = (row // depth) * 8 + below * depth + (row & (depth - 1))
    tag = jnp.zeros((8, width), jnp.float32)
    for column in range(wide):
        for slot in range(8):
            value = order_ref[column, 0, slot].astype(jnp.float32)
            tag = jnp.where(place == column * 8 + slot, value, tag)
    tag_out[...] = tag

    for copy in small[1:]:
        copy.wait()
    filler = jnp.zeros((8 - rows, width), jnp.float32)
    v = jnp.concatenate([first[...].reshape(rows, width), filler], axis=0)
    remainder = jnp.concatenate([rhs[...].reshape(rows, width), filler], axis=0)
    sent[0] = v[0:rows].astype(jnp.bfloat16)

    def halo(groups):
        group = lane // (4 * rows)
        dx, dy = jnp.zeros_like(lane), jnp.zeros_like(lane)
        for g, (x, y) in enumerate(groups):
            dx = jnp.where(group == g, -x, dx)
            dy = jnp.where(group == g, -y, dy)
        inside = (gx + dx >= 0) & (gx + dx < nx) & (gy + dy >= 0) & (gy + dy < ny)
        inside = inside & (lane < 4 * rows * len(groups)) & (own < rows)
        step = wide * dx + (row // depth) - (own // depth)
        return jnp.where(inside & (step >= -1) & (step <= 1), (step + 1) * 3 + dy + 1, -1)

    mine = jnp.full((8, width), -100.0, jnp.float32)
    height = lax.broadcasted_iota(jnp.int32, (8, pattern.shape[-1]), 0)
    keep = jnp.zeros((8, pattern.shape[-1]), jnp.int32)
    for column in range(wide):
        present = pattern[column, 0]
        for slot in range(depth):
            r = column * depth + slot
            mine = jnp.where(own == r, order_ref[column, 0, gz * depth + slot].astype(jnp.float32), mine)
            line = jnp.sum(jnp.where(height == gz * depth + slot, present, 0), axis=0, keepdims=True)
            keep = jnp.where(height == r, line, keep)

    def premask(entries, groups, base):
        flat = halo(groups)
        for j, (low, high) in enumerate(entries):
            chosen = flat == jnp.where(own < depth, low // 3, high // 3)
            if low != 13:
                held = jnp.where(own[:, 0:1] < depth, keep[:, low : low + 1], keep[:, high : high + 1])
                chosen = chosen & (held > 0)
            masks[base + j] = jnp.where(chosen, 1.0, 0.0)

    premask(NEAR_ENTRIES, NEAR, 0)
    premask(FAR_ENTRIES, FAR, len(NEAR_ENTRIES))

    pl.semaphore_wait(barrier, near_peers + far_peers)

    def send(number):
        for groups, buffer, sem in ((FAR, far, far_sem), (NEAR, near, near_sem)):
            for dz in ISSUE:
                for g, (dx, dy) in enumerate(groups):
                    if (dx, dy, dz) == (0, 0, 0):
                        continue
                    slot = 4 * g + TURNS.index(dz)
                    pltpu.make_async_remote_copy(
                        sent.at[number], buffer.at[number, pl.ds(slot * rows, rows)], send_sem.at[number],
                        sem.at[number], device_id=at(dx, dy, dz), device_id_type=MESH,
                    ).start()

    everyone = FAR + NEAR
    for g, (dx, dy) in enumerate(everyone[:-1]):
        pltpu.make_async_remote_copy(
            tag_out, tags.at[g], tag_send, tag_recv, device_id=at(dx, dy, 0), device_id_type=MESH
        ).start()
    send(0)

    load.wait()
    unit = lax.broadcasted_iota(jnp.int32, (width, width), 0) == lax.broadcasted_iota(jnp.int32, (width, width), 1)
    unit = jnp.where(unit, 1.0, 0.0).astype(jnp.bfloat16)

    def turn_block(step, carry):
        for k in range(6):
            block = blocks[6 * step + k]
            flipped = block.T
            turned[6 * step + k] = flipped.astype(jnp.bfloat16)
        return carry

    lax.fori_loop(0, rows * 27 // 6, turn_block, 0)
    others = tags.at[pl.ds(0, len(everyone) - 1)]
    pltpu.make_async_copy(others, others, tag_recv).wait()
    tags[len(everyone) - 1] = tag

    def finish(entries, base, first_tag, count, table):
        plane = jnp.zeros((8, width), jnp.float32)
        for g in range(count):
            plane = jnp.where(lane // (4 * rows) == g, tags[first_tag + g], plane)
        level = [jnp.where(plane == mine + float(c - 1), 1.0, 0.0) for c in range(3)]
        parts = [masks[base + j] * level[low % 3] for j, (low, _) in enumerate(entries)]
        if len(parts) % 2:
            parts.append(jnp.zeros((8, width), jnp.float32))
        for j in range(0, len(parts), 2):
            both = jnp.concatenate(parts[j : j + 2], axis=0)
            table[pl.ds(8 * j, 16), :] = both.astype(jnp.bfloat16)

    finish(NEAR_ENTRIES, 0, len(FAR), len(NEAR), near_table)
    plane = jnp.zeros((8, width), jnp.float32)
    for g in range(len(FAR)):
        plane = jnp.where(lane // (4 * rows) == g, tags[g], plane)
    place = jnp.zeros((8, width), jnp.int32)
    for j, (low, _) in enumerate(FAR_ENTRIES):
        chosen = (masks[len(NEAR_ENTRIES) + j] > 0) & (plane == mine + float(low % 3 - 1))
        spot = jnp.max(jnp.where(chosen, (lane + 8).astype(jnp.float32), 0.0), axis=1, keepdims=True)
        place = jnp.where(lane == j, spot.astype(jnp.int32), place)
    spots[...] = place
    far_rows[pl.ds(0, 8), :] = jnp.zeros((8, width), jnp.float32)
    to_scalars = pltpu.make_async_copy(spots, spot_of, load_sem.at[1])
    to_scalars.start()

    old, new = coefficients()

    def near_rows(number):
        picked = jnp.dot(near_table[:, 0 : 4 * rows * len(NEAR)], near[number], preferred_element_type=jnp.float32)
        parts = [picked[8 * j : 8 * j + 8].astype(jnp.bfloat16) for j in range(len(NEAR_ENTRIES))]
        return [jnp.concatenate(parts, axis=1)] * (rows // depth)

    def diagonal_rows(number):
        far_rows[pl.ds(8, 4 * rows * len(FAR)), :] = far[number].astype(jnp.float32)
        lefts = []
        last = far_rows.shape[0] - 1
        for r in range(0, rows, depth):
            parts = []
            for j in range(len(FAR_ENTRIES)):
                part = jnp.broadcast_to(far_rows[pl.ds(jnp.clip(spot_of[r, j], 0, last), 1), :], (8, width))
                for s in range(1, depth):
                    line = jnp.broadcast_to(far_rows[pl.ds(jnp.clip(spot_of[r + s, j], 0, last), 1), :], (8, width))
                    part = jnp.where(own == r + s, line, part)
                parts.append(part.astype(jnp.bfloat16))
            lefts.append(jnp.concatenate(parts, axis=1))
        return lefts

    def apply(lefts, entries):
        product = jnp.zeros((8, width), jnp.float32)
        for left, r in zip(lefts, range(0, rows, depth)):
            right = jnp.concatenate(
                [
                    jnp.concatenate([turned[(r + s) * 27 + pair[r // depth]] for s in range(depth)], axis=1)
                    for pair in entries
                ],
                axis=0,
            )
            total = jnp.dot(left, right, preferred_element_type=jnp.float32)
            for s in range(depth):
                product = jnp.where(own == r + s, total[:, s * width : (s + 1) * width], product)
        return product

    def turn_of(number, carry):
        v, smoothed, remainder = carry
        a, b = jnp.float32(old[0]), jnp.float32(new[0])
        for i in range(1, DEG):
            a = jnp.where(number == i, jnp.float32(old[i]), a)
            b = jnp.where(number == i, jnp.float32(new[i]), b)
        near[number, pl.ds(near_peers * rows, rows)] = sent[number]
        theirs = near.at[number, pl.ds(0, near_peers * rows)]
        pltpu.make_async_copy(theirs, theirs, near_sem.at[number]).wait()
        partial = remainder - apply(near_rows(number), NEAR_ENTRIES)
        theirs = far.at[number]
        pltpu.make_async_copy(theirs, theirs, far_sem.at[number]).wait()
        remainder = partial - apply(diagonal_rows(number), FAR_ENTRIES)
        following = a * v + b * remainder

        @pl.when(number < DEG)
        def _():
            sent[number + 1] = following[0:rows].astype(jnp.bfloat16)
            send(number + 1)

        return following, smoothed + v, remainder

    to_scalars.wait()
    _, smoothed, remainder = lax.fori_loop(0, DEG + 1, turn_of, (v, jnp.zeros_like(v), remainder))
    out_ref[0] = smoothed[0:rows].reshape(first.shape)
    out_ref[1] = remainder[0:rows].reshape(first.shape)

    pltpu.make_async_copy(others, others, tag_send).wait()

    def drain(number, carry):
        theirs = near.at[number, pl.ds(0, near_peers * rows)]
        pltpu.make_async_copy(theirs, theirs, send_sem.at[number]).wait()
        theirs = far.at[number]
        pltpu.make_async_copy(theirs, theirs, send_sem.at[number]).wait()
        return carry

    lax.fori_loop(0, DEG + 1, drain, 0)


def split(both_ref, smoothed_hbm, remainder_hbm, sem):
    copies = [
        pltpu.make_async_copy(both_ref.at[i], out, sem.at[i]) for i, out in enumerate((smoothed_hbm, remainder_hbm))
    ]
    for copy in copies:
        copy.start()
    for copy in copies:
        copy.wait()


def local(sizes, blocks, pattern, order, start, rhs):
    wide, _, depth, width = start.shape
    rows = wide * depth
    flat = blocks.reshape((rows * blocks.shape[3],) + blocks.shape[4:])
    vmem = pl.BlockSpec(memory_space=pltpu.VMEM)
    anywhere = pl.BlockSpec(memory_space=pl.ANY)
    near_blocks = (len(NEAR_ENTRIES) + 1) // 2
    both = pl.pallas_call(
        functools.partial(kernel, sizes),
        out_shape=pltpu.VMEM((2,) + start.shape, jnp.float32),
        in_specs=[anywhere, anywhere, anywhere, anywhere, anywhere],
        out_specs=vmem,
        scratch_shapes=[
            pltpu.VMEM(flat.shape, jnp.bfloat16),
            pltpu.VMEM(flat.shape, jnp.bfloat16),
            pltpu.SMEM(order.shape, jnp.int32),
            pltpu.VMEM(pattern.shape, jnp.int32),
            pltpu.VMEM(start.shape, jnp.float32),
            pltpu.VMEM(start.shape, jnp.float32),
            pltpu.VMEM((DEG + 1, 4 * rows * len(NEAR), width), jnp.bfloat16),
            pltpu.VMEM((DEG + 1, 4 * rows * len(FAR), width), jnp.bfloat16),
            pltpu.VMEM((DEG + 1, rows, width), jnp.bfloat16),
            pltpu.VMEM((len(NEAR) + len(FAR), 8, width), jnp.float32),
            pltpu.VMEM((8, width), jnp.float32),
            pltpu.VMEM((16 * near_blocks, width), jnp.bfloat16),
            pltpu.VMEM((len(NEAR_ENTRIES) + len(FAR_ENTRIES), 8, width), jnp.float32),
            pltpu.VMEM((8 + 4 * rows * len(FAR), width), jnp.float32),
            pltpu.VMEM((8, width), jnp.int32),
            pltpu.SMEM((8, width), jnp.int32),
            pltpu.SemaphoreType.DMA((5,)),
            pltpu.SemaphoreType.DMA((DEG + 1,)),
            pltpu.SemaphoreType.DMA((DEG + 1,)),
            pltpu.SemaphoreType.DMA((DEG + 1,)),
            pltpu.SemaphoreType.DMA,
            pltpu.SemaphoreType.DMA,
        ],
        compiler_params=pltpu.CompilerParams(collective_id=0, has_side_effects=True),
    )(flat, order, pattern, start, rhs)
    both = pltpu.with_memory_space_constraint(both, pltpu.VMEM)
    piece = jax.ShapeDtypeStruct(start.shape, jnp.float32)
    return pl.pallas_call(
        split,
        out_shape=(piece, piece),
        in_specs=[vmem],
        out_specs=(anywhere, anywhere),
        scratch_shapes=[pltpu.SemaphoreType.DMA((2,))],
    )(both)


def solution(mesh):
    in_specs = (
        P("gx", "gy", "gz", None, None, None),
        P("gx", "gy", None, None),
        P("gx", "gy", None),
        P("gx", "gy", "gz", None),
        P("gx", "gy", "gz", None),
    )
    out_specs = (P("gx", "gy", "gz", None), P("gx", "gy", "gz", None))
    sizes = tuple(mesh.shape[a] for a in ("gx", "gy", "gz"))
    return jax.shard_map(
        functools.partial(local, sizes), mesh=mesh, in_specs=in_specs, out_specs=out_specs, check_vma=False
    )
```

```python
import functools

import jax
import jax.numpy as jnp
from jax import lax
from jax.experimental import pallas as pl
from jax.experimental.pallas import tpu as pltpu
from jax.sharding import PartitionSpec as P

DEG = 4
MESH = pl.DeviceIdType.MESH

NEAR = ((-1, 0), (1, 0), (0, -1), (0, 1), (0, 0))
FAR = ((1, 1), (-1, -1), (1, -1), (-1, 1))
TURNS = (1, 2, 3, 0)
ISSUE = (2, 1, 3, 0)
NEAR_ENTRIES = [(9 * a + 3 * b + c, 9 * d + 3 * b + c) for a, d in ((1, 1), (2, 0)) for b in range(3) for c in range(3)]
NEAR_ENTRIES += [(3 + c, 21 + c) for c in range(3)]
FAR_ENTRIES = [(3 * b + c, 18 + 3 * b + c) for b in (0, 2) for c in range(3)]


def coefficients():
    center, spread = 1.0, 0.8
    sigma = center / spread
    rho = 1.0 / sigma
    old, new = [0.0], [1.0 / center]
    for _ in range(DEG - 1):
        following = 1.0 / (2.0 * sigma - rho)
        old.append(following * rho)
        new.append(2.0 * following / spread)
        rho = following
    return old, new


def kernel(sizes, blocks_hbm, order_hbm, pattern_hbm, start_hbm, rhs_hbm, out_ref,
           blocks, turned, order_ref, pattern, first, rhs, near, far, sent, tags, tag_out, near_table, masks, far_rows, spots, spot_of,
           load_sem, send_sem, near_sem, far_sem, tag_send, tag_recv):
    nx, ny, nz = sizes
    gx, gy, gz = (lax.axis_index(a) for a in ("gx", "gy", "gz"))
    wide, _, depth, width = first.shape
    rows = wide * depth
    near_peers, far_peers = 4 * len(NEAR) - 1, 4 * len(FAR)

    def at(dx, dy, dz):
        return (lax.rem(gx + (dx + nx), nx), lax.rem(gy + (dy + ny), ny), lax.rem(gz + dz, nz))

    barrier = pltpu.get_barrier_semaphore()
    for dz in ISSUE:
        for dx, dy in FAR + NEAR:
            if (dx, dy, dz) != (0, 0, 0):
                pl.semaphore_signal(barrier, inc=1, device_id=at(dx, dy, dz), device_id_type=MESH)

    small = [
        pltpu.make_async_copy(a, b, load_sem.at[1 + i])
        for i, (a, b) in enumerate(((order_hbm, order_ref), (start_hbm, first), (rhs_hbm, rhs), (pattern_hbm, pattern)))
    ]
    for copy in small:
        copy.start()
    load = pltpu.make_async_copy(blocks_hbm, blocks, load_sem.at[0])
    load.start()

    small[0].wait()
    lane = lax.broadcasted_iota(jnp.int32, (8, width), 1)
    own = lax.broadcasted_iota(jnp.int32, (8, width), 0)
    period = lane & (4 * rows - 1)
    row = period & (rows - 1)
    below = (gz + 3 - period // rows) & (nz - 1)
    place = (row // depth) * 8 + below * depth + (row & (depth - 1))
    tag = jnp.zeros((8, width), jnp.float32)
    for column in range(wide):
        for slot in range(8):
            value = order_ref[column, 0, slot].astype(jnp.float32)
            tag = jnp.where(place == column * 8 + slot, value, tag)
    tag_out[...] = tag

    for copy in small[1:]:
        copy.wait()
    filler = jnp.zeros((8 - rows, width), jnp.float32)
    v = jnp.concatenate([first[...].reshape(rows, width), filler], axis=0)
    remainder = jnp.concatenate([rhs[...].reshape(rows, width), filler], axis=0)
    sent[0] = v[0:rows].astype(jnp.bfloat16)

    def halo(groups):
        group = lane // (4 * rows)
        dx, dy = jnp.zeros_like(lane), jnp.zeros_like(lane)
        for g, (x, y) in enumerate(groups):
            dx = jnp.where(group == g, -x, dx)
            dy = jnp.where(group == g, -y, dy)
        inside = (gx + dx >= 0) & (gx + dx < nx) & (gy + dy >= 0) & (gy + dy < ny)
        inside = inside & (lane < 4 * rows * len(groups)) & (own < rows)
        step = wide * dx + (row // depth) - (own // depth)
        return jnp.where(inside & (step >= -1) & (step <= 1), (step + 1) * 3 + dy + 1, -1)

    mine = jnp.full((8, width), -100.0, jnp.float32)
    height = lax.broadcasted_iota(jnp.int32, (8, pattern.shape[-1]), 0)
    keep = jnp.zeros((8, pattern.shape[-1]), jnp.int32)
    for column in range(wide):
        present = pattern[column, 0]
        for slot in range(depth):
            r = column * depth + slot
            mine = jnp.where(own == r, order_ref[column, 0, gz * depth + slot].astype(jnp.float32), mine)
            line = jnp.sum(jnp.where(height == gz * depth + slot, present, 0), axis=0, keepdims=True)
            keep = jnp.where(height == r, line, keep)

    def premask(entries, groups, base):
        flat = halo(groups)
        for j, (low, high) in enumerate(entries):
            chosen = flat == jnp.where(own < depth, low // 3, high // 3)
            if low != 13:
                held = jnp.where(own[:, 0:1] < depth, keep[:, low : low + 1], keep[:, high : high + 1])
                chosen = chosen & (held > 0)
            masks[base + j] = jnp.where(chosen, 1.0, 0.0)

    premask(NEAR_ENTRIES, NEAR, 0)
    premask(FAR_ENTRIES, FAR, len(NEAR_ENTRIES))

    pl.semaphore_wait(barrier, near_peers + far_peers)

    def send(number):
        for groups, buffer, sem in ((FAR, far, far_sem), (NEAR, near, near_sem)):
            for dz in ISSUE:
                for g, (dx, dy) in enumerate(groups):
                    if (dx, dy, dz) == (0, 0, 0):
                        continue
                    slot = 4 * g + TURNS.index(dz)
                    pltpu.make_async_remote_copy(
                        sent.at[number], buffer.at[number, pl.ds(slot * rows, rows)], send_sem.at[number],
                        sem.at[number], device_id=at(dx, dy, dz), device_id_type=MESH,
                    ).start()

    everyone = FAR + NEAR
    for g, (dx, dy) in enumerate(everyone[:-1]):
        pltpu.make_async_remote_copy(
            tag_out, tags.at[g], tag_send, tag_recv, device_id=at(dx, dy, 0), device_id_type=MESH
        ).start()
    send(0)

    load.wait()
    unit = lax.broadcasted_iota(jnp.int32, (width, width), 0) == lax.broadcasted_iota(jnp.int32, (width, width), 1)
    unit = jnp.where(unit, 1.0, 0.0).astype(jnp.bfloat16)

    def turn_block(step, carry):
        for k in range(6):
            block = blocks[6 * step + k]
            flipped = block.T
            turned[6 * step + k] = flipped.astype(jnp.bfloat16)
        return carry

    lax.fori_loop(0, rows * 27 // 6, turn_block, 0)
    others = tags.at[pl.ds(0, len(everyone) - 1)]
    pltpu.make_async_copy(others, others, tag_recv).wait()
    tags[len(everyone) - 1] = tag

    def finish(entries, base, first_tag, count, table):
        plane = jnp.zeros((8, width), jnp.float32)
        for g in range(count):
            plane = jnp.where(lane // (4 * rows) == g, tags[first_tag + g], plane)
        level = [jnp.where(plane == mine + float(c - 1), 1.0, 0.0) for c in range(3)]
        parts = [masks[base + j] * level[low % 3] for j, (low, _) in enumerate(entries)]
        if len(parts) % 2:
            parts.append(jnp.zeros((8, width), jnp.float32))
        for j in range(0, len(parts), 2):
            both = jnp.concatenate(parts[j : j + 2], axis=0)
            table[pl.ds(8 * j, 16), :] = both.astype(jnp.bfloat16)

    finish(NEAR_ENTRIES, 0, len(FAR), len(NEAR), near_table)
    plane = jnp.zeros((8, width), jnp.float32)
    for g in range(len(FAR)):
        plane = jnp.where(lane // (4 * rows) == g, tags[g], plane)
    place = jnp.zeros((8, width), jnp.int32)
    for j, (low, _) in enumerate(FAR_ENTRIES):
        chosen = (masks[len(NEAR_ENTRIES) + j] > 0) & (plane == mine + float(low % 3 - 1))
        spot = jnp.max(jnp.where(chosen, (lane + 8).astype(jnp.float32), 0.0), axis=1, keepdims=True)
        place = jnp.where(lane == j, spot.astype(jnp.int32), place)
    spots[...] = place
    far_rows[pl.ds(0, 8), :] = jnp.zeros((8, width), jnp.float32)
    to_scalars = pltpu.make_async_copy(spots, spot_of, load_sem.at[1])
    to_scalars.start()

    old, new = coefficients()

    def weights(entries, r, first):
        pairs = entries[first : first + 2]
        blocks_of = [
            jnp.concatenate([turned[(r + s) * 27 + pair[r // depth]] for s in range(depth)], axis=1) for pair in pairs
        ]
        if len(pairs) == 1:
            blocks_of.append(jnp.zeros((width, 2 * width), jnp.bfloat16))
        return jnp.concatenate(blocks_of, axis=0)

    def own_rows(totals):
        product = jnp.zeros((8, width), jnp.float32)
        for total, r in zip(totals, range(0, rows, depth)):
            for s in range(depth):
                product = jnp.where(own == r + s, total[:, s * width : (s + 1) * width], product)
        return product

    def nearby(number, picked_0, unit_0, unit_1):
        seen = near[number]
        seen = jnp.concatenate([seen, jnp.zeros((2 * width - seen.shape[0], width), jnp.bfloat16)], axis=0)
        pltpu.matmul_push_rhs(jnp.concatenate([seen, jnp.zeros_like(seen)], axis=1), 0, 0)
        units = list(zip((unit_0, unit_1), range(0, rows, depth)))
        pltpu.matmul_push_rhs(weights(NEAR_ENTRIES, units[1][1], 0), 0, 1)
        table = near_table[...]
        pltpu.matmul_acc_lhs(picked_0, jnp.concatenate([table, jnp.zeros_like(table)], axis=1), 0)
        pltpu.matmul_push_rhs(weights(NEAR_ENTRIES, units[0][1], 0), 0, 0)
        picked = pltpu.matmul_pop(picked_0)[:, 0:width]
        chunks = range(0, len(NEAR_ENTRIES), 2)
        for n, first in enumerate(chunks):
            left = jnp.concatenate([picked[8 * first : 8 * first + 8], picked[8 * first + 8 : 8 * first + 16]], axis=1)
            left = jnp.concatenate([left, jnp.zeros_like(left)], axis=0).astype(jnp.bfloat16)
            for i, (acc, r) in enumerate(units):
                if n + 1 < len(chunks):
                    pltpu.matmul_push_rhs(weights(NEAR_ENTRIES, r, first + 2), (n + 1) % 2, i)
                pltpu.matmul_acc_lhs(acc, left, n % 2)
        return own_rows([pltpu.matmul_pop(acc)[0:8] for acc, _ in units])

    def diagonal_row(r, j):
        last = far_rows.shape[0] - 1
        part = jnp.broadcast_to(far_rows[pl.ds(jnp.clip(spot_of[r, j], 0, last), 1), :], (8, width))
        for s in range(1, depth):
            line = jnp.broadcast_to(far_rows[pl.ds(jnp.clip(spot_of[r + s, j], 0, last), 1), :], (8, width))
            part = jnp.where(own == r + s, line, part)
        return part

    def diagonal_left(r, first):
        left = jnp.concatenate([diagonal_row(r, first), diagonal_row(r, first + 1)], axis=1)
        return jnp.concatenate([left, jnp.zeros_like(left)], axis=0).astype(jnp.bfloat16)

    def diagonal(number, unit_0, unit_1):
        units = list(zip((unit_0, unit_1), range(0, rows, depth)))
        for i, (_, r) in enumerate(units):
            pltpu.matmul_push_rhs(weights(FAR_ENTRIES, r, 0), 0, i)
            pltpu.matmul_push_rhs(weights(FAR_ENTRIES, r, 2), 1, i)
        theirs = far.at[number]
        pltpu.make_async_copy(theirs, theirs, far_sem.at[number]).wait()
        far_rows[pl.ds(8, 4 * rows * len(FAR)), :] = far[number].astype(jnp.float32)
        for i, (acc, r) in enumerate(units):
            pltpu.matmul_acc_lhs(acc, diagonal_left(r, 0), 0)
            pltpu.matmul_push_rhs(weights(FAR_ENTRIES, r, 4), 0, i)
        for i, (acc, r) in enumerate(units):
            pltpu.matmul_acc_lhs(acc, diagonal_left(r, 2), 1)
            pltpu.matmul_acc_lhs(acc, diagonal_left(r, 4), 0)
        return own_rows([pltpu.matmul_pop(acc)[0:8] for acc, _ in units])

    def turn_of(number, carry):
        v, smoothed, remainder = carry
        a, b = jnp.float32(old[0]), jnp.float32(new[0])
        for i in range(1, DEG):
            a = jnp.where(number == i, jnp.float32(old[i]), a)
            b = jnp.where(number == i, jnp.float32(new[i]), b)
        near[number, pl.ds(near_peers * rows, rows)] = sent[number]
        theirs = near.at[number, pl.ds(0, near_peers * rows)]
        pltpu.make_async_copy(theirs, theirs, near_sem.at[number]).wait()
        partial = remainder - pl.run_scoped(
            functools.partial(nearby, number),
            pltpu.ACC(0)((near_table.shape[0], 2 * width), jnp.float32),
            pltpu.ACC(0)((16, 2 * width), jnp.float32),
            pltpu.ACC(1)((16, 2 * width), jnp.float32),
        )
        remainder = partial - pl.run_scoped(
            functools.partial(diagonal, number),
            pltpu.ACC(0)((16, 2 * width), jnp.float32),
            pltpu.ACC(1)((16, 2 * width), jnp.float32),
        )
        following = a * v + b * remainder

        @pl.when(number < DEG)
        def _():
            sent[number + 1] = following[0:rows].astype(jnp.bfloat16)
            send(number + 1)

        return following, smoothed + v, remainder

    to_scalars.wait()
    _, smoothed, remainder = lax.fori_loop(0, DEG + 1, turn_of, (v, jnp.zeros_like(v), remainder))
    out_ref[0] = smoothed[0:rows].reshape(first.shape)
    out_ref[1] = remainder[0:rows].reshape(first.shape)

    pltpu.make_async_copy(others, others, tag_send).wait()

    def drain(number, carry):
        theirs = near.at[number, pl.ds(0, near_peers * rows)]
        pltpu.make_async_copy(theirs, theirs, send_sem.at[number]).wait()
        theirs = far.at[number]
        pltpu.make_async_copy(theirs, theirs, send_sem.at[number]).wait()
        return carry

    lax.fori_loop(0, DEG + 1, drain, 0)


def split(both_ref, smoothed_hbm, remainder_hbm, sem):
    copies = [
        pltpu.make_async_copy(both_ref.at[i], out, sem.at[i]) for i, out in enumerate((smoothed_hbm, remainder_hbm))
    ]
    for copy in copies:
        copy.start()
    for copy in copies:
        copy.wait()


def local(sizes, blocks, pattern, order, start, rhs):
    wide, _, depth, width = start.shape
    rows = wide * depth
    flat = blocks.reshape((rows * blocks.shape[3],) + blocks.shape[4:])
    vmem = pl.BlockSpec(memory_space=pltpu.VMEM)
    anywhere = pl.BlockSpec(memory_space=pl.ANY)
    near_blocks = (len(NEAR_ENTRIES) + 1) // 2
    both = pl.pallas_call(
        functools.partial(kernel, sizes),
        out_shape=pltpu.VMEM((2,) + start.shape, jnp.float32),
        in_specs=[anywhere, anywhere, anywhere, anywhere, anywhere],
        out_specs=vmem,
        scratch_shapes=[
            pltpu.VMEM(flat.shape, jnp.bfloat16),
            pltpu.VMEM(flat.shape, jnp.bfloat16),
            pltpu.SMEM(order.shape, jnp.int32),
            pltpu.VMEM(pattern.shape, jnp.int32),
            pltpu.VMEM(start.shape, jnp.float32),
            pltpu.VMEM(start.shape, jnp.float32),
            pltpu.VMEM((DEG + 1, 4 * rows * len(NEAR), width), jnp.bfloat16),
            pltpu.VMEM((DEG + 1, 4 * rows * len(FAR), width), jnp.bfloat16),
            pltpu.VMEM((DEG + 1, rows, width), jnp.bfloat16),
            pltpu.VMEM((len(NEAR) + len(FAR), 8, width), jnp.float32),
            pltpu.VMEM((8, width), jnp.float32),
            pltpu.VMEM((16 * near_blocks, width), jnp.bfloat16),
            pltpu.VMEM((len(NEAR_ENTRIES) + len(FAR_ENTRIES), 8, width), jnp.float32),
            pltpu.VMEM((8 + 4 * rows * len(FAR), width), jnp.float32),
            pltpu.VMEM((8, width), jnp.int32),
            pltpu.SMEM((8, width), jnp.int32),
            pltpu.SemaphoreType.DMA((5,)),
            pltpu.SemaphoreType.DMA((DEG + 1,)),
            pltpu.SemaphoreType.DMA((DEG + 1,)),
            pltpu.SemaphoreType.DMA((DEG + 1,)),
            pltpu.SemaphoreType.DMA,
            pltpu.SemaphoreType.DMA,
        ],
        compiler_params=pltpu.CompilerParams(collective_id=0, has_side_effects=True),
    )(flat, order, pattern, start, rhs)
    both = pltpu.with_memory_space_constraint(both, pltpu.VMEM)
    piece = jax.ShapeDtypeStruct(start.shape, jnp.float32)
    return pl.pallas_call(
        split,
        out_shape=(piece, piece),
        in_specs=[vmem],
        out_specs=(anywhere, anywhere),
        scratch_shapes=[pltpu.SemaphoreType.DMA((2,))],
    )(both)


def solution(mesh):
    in_specs = (
        P("gx", "gy", "gz", None, None, None),
        P("gx", "gy", None, None),
        P("gx", "gy", None),
        P("gx", "gy", "gz", None),
        P("gx", "gy", "gz", None),
    )
    out_specs = (P("gx", "gy", "gz", None), P("gx", "gy", "gz", None))
    sizes = tuple(mesh.shape[a] for a in ("gx", "gy", "gz"))
    return jax.shard_map(
        functools.partial(local, sizes), mesh=mesh, in_specs=in_specs, out_specs=out_specs, check_vma=False
    )
```

```python
import functools

import jax
import jax.numpy as jnp
from jax import lax
from jax.experimental import pallas as pl
from jax.experimental.pallas import tpu as pltpu
from jax.sharding import PartitionSpec as P

DEG = 4
MESH = pl.DeviceIdType.MESH

NEAR = ((-1, 0), (1, 0), (0, -1), (0, 1), (0, 0))
FAR = ((1, 1), (-1, -1), (1, -1), (-1, 1))
TURNS = (1, 2, 3, 0)
ISSUE = (2, 1, 3, 0)
NEAR_ENTRIES = [(9 * a + 3 * b + c, 9 * d + 3 * b + c) for a, d in ((1, 1), (2, 0)) for b in range(3) for c in range(3)]
NEAR_ENTRIES += [(3 + c, 21 + c) for c in range(3)]
FAR_ENTRIES = [(3 * b + c, 18 + 3 * b + c) for b in (0, 2) for c in range(3)]


def coefficients():
    center, spread = 1.0, 0.8
    sigma = center / spread
    rho = 1.0 / sigma
    old, new = [0.0], [1.0 / center]
    for _ in range(DEG - 1):
        following = 1.0 / (2.0 * sigma - rho)
        old.append(following * rho)
        new.append(2.0 * following / spread)
        rho = following
    return old, new


def kernel(sizes, blocks_hbm, order_hbm, pattern_hbm, start_hbm, rhs_hbm, out_ref,
           blocks, turned, order_ref, pattern, first, rhs, near, far, sent, tags, tag_out, near_table, masks, far_rows, spots, spot_of,
           load_sem, send_sem, near_sem, far_sem, tag_send, tag_recv):
    nx, ny, nz = sizes
    gx, gy, gz = (lax.axis_index(a) for a in ("gx", "gy", "gz"))
    wide, _, depth, width = first.shape
    rows = wide * depth
    near_peers, far_peers = 4 * len(NEAR) - 1, 4 * len(FAR)

    def at(dx, dy, dz):
        return (lax.rem(gx + (dx + nx), nx), lax.rem(gy + (dy + ny), ny), lax.rem(gz + dz, nz))

    barrier = pltpu.get_barrier_semaphore()
    for dz in ISSUE:
        for dx, dy in FAR + NEAR:
            if (dx, dy, dz) != (0, 0, 0):
                pl.semaphore_signal(barrier, inc=1, device_id=at(dx, dy, dz), device_id_type=MESH)

    small = [
        pltpu.make_async_copy(a, b, load_sem.at[1 + i])
        for i, (a, b) in enumerate(((order_hbm, order_ref), (start_hbm, first), (rhs_hbm, rhs), (pattern_hbm, pattern)))
    ]
    for copy in small:
        copy.start()
    load = pltpu.make_async_copy(blocks_hbm, blocks, load_sem.at[0])
    load.start()

    small[0].wait()
    lane = lax.broadcasted_iota(jnp.int32, (8, width), 1)
    own = lax.broadcasted_iota(jnp.int32, (8, width), 0)
    period = lane & (4 * rows - 1)
    row = period & (rows - 1)
    below = (gz + 3 - period // rows) & (nz - 1)
    place = (row // depth) * 8 + below * depth + (row & (depth - 1))
    tag = jnp.zeros((8, width), jnp.float32)
    for column in range(wide):
        for slot in range(8):
            value = order_ref[column, 0, slot].astype(jnp.float32)
            tag = jnp.where(place == column * 8 + slot, value, tag)
    tag_out[...] = tag

    for copy in small[1:]:
        copy.wait()
    filler = jnp.zeros((8 - rows, width), jnp.float32)
    v = jnp.concatenate([first[...].reshape(rows, width), filler], axis=0)
    remainder = jnp.concatenate([rhs[...].reshape(rows, width), filler], axis=0)
    sent[0] = v[0:rows].astype(jnp.bfloat16)

    def halo(groups):
        group = lane // (4 * rows)
        dx, dy = jnp.zeros_like(lane), jnp.zeros_like(lane)
        for g, (x, y) in enumerate(groups):
            dx = jnp.where(group == g, -x, dx)
            dy = jnp.where(group == g, -y, dy)
        inside = (gx + dx >= 0) & (gx + dx < nx) & (gy + dy >= 0) & (gy + dy < ny)
        inside = inside & (lane < 4 * rows * len(groups)) & (own < rows)
        step = wide * dx + (row // depth) - (own // depth)
        return jnp.where(inside & (step >= -1) & (step <= 1), (step + 1) * 3 + dy + 1, -1)

    mine = jnp.full((8, width), -100.0, jnp.float32)
    height = lax.broadcasted_iota(jnp.int32, (8, pattern.shape[-1]), 0)
    keep = jnp.zeros((8, pattern.shape[-1]), jnp.int32)
    for column in range(wide):
        present = pattern[column, 0]
        for slot in range(depth):
            r = column * depth + slot
            mine = jnp.where(own == r, order_ref[column, 0, gz * depth + slot].astype(jnp.float32), mine)
            line = jnp.sum(jnp.where(height == gz * depth + slot, present, 0), axis=0, keepdims=True)
            keep = jnp.where(height == r, line, keep)

    def premask(entries, groups, base):
        flat = halo(groups)
        for j, (low, high) in enumerate(entries):
            chosen = flat == jnp.where(own < depth, low // 3, high // 3)
            if low != 13:
                held = jnp.where(own[:, 0:1] < depth, keep[:, low : low + 1], keep[:, high : high + 1])
                chosen = chosen & (held > 0)
            masks[base + j] = jnp.where(chosen, 1.0, 0.0)

    premask(NEAR_ENTRIES, NEAR, 0)
    premask(FAR_ENTRIES, FAR, len(NEAR_ENTRIES))

    pl.semaphore_wait(barrier, near_peers + far_peers)

    def send(number):
        for groups, buffer, sem in ((FAR, far, far_sem), (NEAR, near, near_sem)):
            for dz in ISSUE:
                for g, (dx, dy) in enumerate(groups):
                    if (dx, dy, dz) == (0, 0, 0):
                        continue
                    slot = 4 * g + TURNS.index(dz)
                    pltpu.make_async_remote_copy(
                        sent.at[number], buffer.at[number, pl.ds(slot * rows, rows)], send_sem.at[number],
                        sem.at[number], device_id=at(dx, dy, dz), device_id_type=MESH,
                    ).start()

    everyone = FAR + NEAR
    for g, (dx, dy) in enumerate(everyone[:-1]):
        pltpu.make_async_remote_copy(
            tag_out, tags.at[g], tag_send, tag_recv, device_id=at(dx, dy, 0), device_id_type=MESH
        ).start()
    send(0)

    load.wait()
    unit = lax.broadcasted_iota(jnp.int32, (width, width), 0) == lax.broadcasted_iota(jnp.int32, (width, width), 1)
    unit = jnp.where(unit, 1.0, 0.0).astype(jnp.bfloat16)

    def turn_block(step, carry):
        for k in range(6):
            block = blocks[6 * step + k]
            flipped = block.T
            turned[6 * step + k] = flipped.astype(jnp.bfloat16)
        return carry

    lax.fori_loop(0, rows * 27 // 6, turn_block, 0)
    others = tags.at[pl.ds(0, len(everyone) - 1)]
    pltpu.make_async_copy(others, others, tag_recv).wait()
    tags[len(everyone) - 1] = tag

    def finish(entries, base, first_tag, count, table):
        plane = jnp.zeros((8, width), jnp.float32)
        for g in range(count):
            plane = jnp.where(lane // (4 * rows) == g, tags[first_tag + g], plane)
        level = [jnp.where(plane == mine + float(c - 1), 1.0, 0.0) for c in range(3)]
        parts = [masks[base + j] * level[low % 3] for j, (low, _) in enumerate(entries)]
        if len(parts) % 2:
            parts.append(jnp.zeros((8, width), jnp.float32))
        for j in range(0, len(parts), 2):
            both = jnp.concatenate(parts[j : j + 2], axis=0)
            table[pl.ds(8 * j, 16), :] = both.astype(jnp.bfloat16)

    finish(NEAR_ENTRIES, 0, len(FAR), len(NEAR), near_table)
    plane = jnp.zeros((8, width), jnp.float32)
    for g in range(len(FAR)):
        plane = jnp.where(lane // (4 * rows) == g, tags[g], plane)
    place = jnp.zeros((8, width), jnp.int32)
    for j, (low, _) in enumerate(FAR_ENTRIES):
        chosen = (masks[len(NEAR_ENTRIES) + j] > 0) & (plane == mine + float(low % 3 - 1))
        spot = jnp.max(jnp.where(chosen, (lane + 8).astype(jnp.float32), 0.0), axis=1, keepdims=True)
        place = jnp.where(lane == j, spot.astype(jnp.int32), place)
    spots[...] = place
    far_rows[pl.ds(0, 8), :] = jnp.zeros((8, width), jnp.float32)
    to_scalars = pltpu.make_async_copy(spots, spot_of, load_sem.at[1])
    to_scalars.start()

    old, new = coefficients()

    def weights(entries, r, first):
        pairs = entries[first : first + 2]
        blocks_of = [
            jnp.concatenate([turned[(r + s) * 27 + pair[r // depth]] for s in range(depth)], axis=1) for pair in pairs
        ]
        if len(pairs) == 1:
            blocks_of.append(jnp.zeros((width, 2 * width), jnp.bfloat16))
        return jnp.concatenate(blocks_of, axis=0)

    def own_rows(totals):
        product = jnp.zeros((8, width), jnp.float32)
        for total, r in zip(totals, range(0, rows, depth)):
            for s in range(depth):
                product = jnp.where(own == r + s, total[:, s * width : (s + 1) * width], product)
        return product

    def nearby(number, picked_0, unit_0, unit_1):
        seen = near[number]
        seen = jnp.concatenate([seen, jnp.zeros((2 * width - seen.shape[0], width), jnp.bfloat16)], axis=0)
        pltpu.matmul_push_rhs(jnp.concatenate([seen, jnp.zeros_like(seen)], axis=1), 0, 0)
        units = list(zip((unit_0, unit_1), range(0, rows, depth)))
        pltpu.matmul_push_rhs(weights(NEAR_ENTRIES, units[1][1], 0), 0, 1)
        table = near_table[...]
        pltpu.matmul_acc_lhs(picked_0, jnp.concatenate([table, jnp.zeros_like(table)], axis=1), 0)
        pltpu.matmul_push_rhs(weights(NEAR_ENTRIES, units[0][1], 0), 0, 0)
        picked = pltpu.matmul_pop(picked_0)[:, 0:width]
        chunks = range(0, len(NEAR_ENTRIES), 2)
        for n, first in enumerate(chunks):
            left = jnp.concatenate([picked[8 * first : 8 * first + 8], picked[8 * first + 8 : 8 * first + 16]], axis=1)
            left = jnp.concatenate([left, jnp.zeros_like(left)], axis=0).astype(jnp.bfloat16)
            for i, (acc, r) in enumerate(units):
                if n + 1 < len(chunks):
                    pltpu.matmul_push_rhs(weights(NEAR_ENTRIES, r, first + 2), (n + 1) % 2, i)
                pltpu.matmul_acc_lhs(acc, left, n % 2)
        return own_rows([pltpu.matmul_pop(acc)[0:8] for acc, _ in units])

    def diagonal_row(spots_now, r, j):
        part = jnp.broadcast_to(far_rows[pl.ds(spots_now[r][j], 1), :], (8, width))
        for s in range(1, depth):
            line = jnp.broadcast_to(far_rows[pl.ds(spots_now[r + s][j], 1), :], (8, width))
            part = jnp.where(own == r + s, line, part)
        return part

    def diagonal_left(spots_now, r, first):
        left = jnp.concatenate([diagonal_row(spots_now, r, first), diagonal_row(spots_now, r, first + 1)], axis=1)
        return jnp.concatenate([left, jnp.zeros_like(left)], axis=0).astype(jnp.bfloat16)

    def diagonal(number, unit_0, unit_1):
        units = list(zip((unit_0, unit_1), range(0, rows, depth)))
        for i, (_, r) in enumerate(units):
            pltpu.matmul_push_rhs(weights(FAR_ENTRIES, r, 0), 0, i)
            pltpu.matmul_push_rhs(weights(FAR_ENTRIES, r, 2), 1, i)
        last = far_rows.shape[0] - 1
        spots_now = [[jnp.clip(spot_of[r, j], 0, last) for j in range(len(FAR_ENTRIES))] for r in range(rows)]
        theirs = far.at[number]
        pltpu.make_async_copy(theirs, theirs, far_sem.at[number]).wait()
        far_rows[pl.ds(8, 4 * rows * len(FAR)), :] = far[number].astype(jnp.float32)
        for i, (acc, r) in enumerate(units):
            pltpu.matmul_acc_lhs(acc, diagonal_left(spots_now, r, 0), 0)
            pltpu.matmul_push_rhs(weights(FAR_ENTRIES, r, 4), 0, i)
        for i, (acc, r) in enumerate(units):
            pltpu.matmul_acc_lhs(acc, diagonal_left(spots_now, r, 2), 1)
            pltpu.matmul_acc_lhs(acc, diagonal_left(spots_now, r, 4), 0)
        return own_rows([pltpu.matmul_pop(acc)[0:8] for acc, _ in units])

    def turn_of(number, carry):
        v, smoothed, remainder = carry
        a, b = jnp.float32(old[0]), jnp.float32(new[0])
        for i in range(1, DEG):
            a = jnp.where(number == i, jnp.float32(old[i]), a)
            b = jnp.where(number == i, jnp.float32(new[i]), b)
        near[number, pl.ds(near_peers * rows, rows)] = sent[number]
        theirs = near.at[number, pl.ds(0, near_peers * rows)]
        pltpu.make_async_copy(theirs, theirs, near_sem.at[number]).wait()
        partial = remainder - pl.run_scoped(
            functools.partial(nearby, number),
            pltpu.ACC(0)((near_table.shape[0], 2 * width), jnp.float32),
            pltpu.ACC(0)((16, 2 * width), jnp.float32),
            pltpu.ACC(1)((16, 2 * width), jnp.float32),
        )
        remainder = partial - pl.run_scoped(
            functools.partial(diagonal, number),
            pltpu.ACC(0)((16, 2 * width), jnp.float32),
            pltpu.ACC(1)((16, 2 * width), jnp.float32),
        )
        following = a * v + b * remainder

        @pl.when(number < DEG)
        def _():
            sent[number + 1] = following[0:rows].astype(jnp.bfloat16)
            send(number + 1)

        return following, smoothed + v, remainder

    to_scalars.wait()
    _, smoothed, remainder = lax.fori_loop(0, DEG + 1, turn_of, (v, jnp.zeros_like(v), remainder))
    out_ref[0] = smoothed[0:rows].reshape(first.shape)
    out_ref[1] = remainder[0:rows].reshape(first.shape)

    pltpu.make_async_copy(others, others, tag_send).wait()

    def drain(number, carry):
        theirs = near.at[number, pl.ds(0, near_peers * rows)]
        pltpu.make_async_copy(theirs, theirs, send_sem.at[number]).wait()
        theirs = far.at[number]
        pltpu.make_async_copy(theirs, theirs, send_sem.at[number]).wait()
        return carry

    lax.fori_loop(0, DEG + 1, drain, 0)


def split(both_ref, smoothed_hbm, remainder_hbm, sem):
    copies = [
        pltpu.make_async_copy(both_ref.at[i], out, sem.at[i]) for i, out in enumerate((smoothed_hbm, remainder_hbm))
    ]
    for copy in copies:
        copy.start()
    for copy in copies:
        copy.wait()


def local(sizes, blocks, pattern, order, start, rhs):
    wide, _, depth, width = start.shape
    rows = wide * depth
    flat = blocks.reshape((rows * blocks.shape[3],) + blocks.shape[4:])
    vmem = pl.BlockSpec(memory_space=pltpu.VMEM)
    anywhere = pl.BlockSpec(memory_space=pl.ANY)
    near_blocks = (len(NEAR_ENTRIES) + 1) // 2
    both = pl.pallas_call(
        functools.partial(kernel, sizes),
        out_shape=pltpu.VMEM((2,) + start.shape, jnp.float32),
        in_specs=[anywhere, anywhere, anywhere, anywhere, anywhere],
        out_specs=vmem,
        scratch_shapes=[
            pltpu.VMEM(flat.shape, jnp.bfloat16),
            pltpu.VMEM(flat.shape, jnp.bfloat16),
            pltpu.SMEM(order.shape, jnp.int32),
            pltpu.VMEM(pattern.shape, jnp.int32),
            pltpu.VMEM(start.shape, jnp.float32),
            pltpu.VMEM(start.shape, jnp.float32),
            pltpu.VMEM((DEG + 1, 4 * rows * len(NEAR), width), jnp.bfloat16),
            pltpu.VMEM((DEG + 1, 4 * rows * len(FAR), width), jnp.bfloat16),
            pltpu.VMEM((DEG + 1, rows, width), jnp.bfloat16),
            pltpu.VMEM((len(NEAR) + len(FAR), 8, width), jnp.float32),
            pltpu.VMEM((8, width), jnp.float32),
            pltpu.VMEM((16 * near_blocks, width), jnp.bfloat16),
            pltpu.VMEM((len(NEAR_ENTRIES) + len(FAR_ENTRIES), 8, width), jnp.float32),
            pltpu.VMEM((8 + 4 * rows * len(FAR), width), jnp.float32),
            pltpu.VMEM((8, width), jnp.int32),
            pltpu.SMEM((8, width), jnp.int32),
            pltpu.SemaphoreType.DMA((5,)),
            pltpu.SemaphoreType.DMA((DEG + 1,)),
            pltpu.SemaphoreType.DMA((DEG + 1,)),
            pltpu.SemaphoreType.DMA((DEG + 1,)),
            pltpu.SemaphoreType.DMA,
            pltpu.SemaphoreType.DMA,
        ],
        compiler_params=pltpu.CompilerParams(collective_id=0, has_side_effects=True),
    )(flat, order, pattern, start, rhs)
    both = pltpu.with_memory_space_constraint(both, pltpu.VMEM)
    piece = jax.ShapeDtypeStruct(start.shape, jnp.float32)
    return pl.pallas_call(
        split,
        out_shape=(piece, piece),
        in_specs=[vmem],
        out_specs=(anywhere, anywhere),
        scratch_shapes=[pltpu.SemaphoreType.DMA((2,))],
    )(both)


def solution(mesh):
    in_specs = (
        P("gx", "gy", "gz", None, None, None),
        P("gx", "gy", None, None),
        P("gx", "gy", None),
        P("gx", "gy", "gz", None),
        P("gx", "gy", "gz", None),
    )
    out_specs = (P("gx", "gy", "gz", None), P("gx", "gy", "gz", None))
    sizes = tuple(mesh.shape[a] for a in ("gx", "gy", "gz"))
    return jax.shard_map(
        functools.partial(local, sizes), mesh=mesh, in_specs=in_specs, out_specs=out_specs, check_vma=False
    )
```

```python
import functools

import jax
import jax.numpy as jnp
from jax import lax
from jax.experimental import pallas as pl
from jax.experimental.pallas import tpu as pltpu
from jax.sharding import PartitionSpec as P

DEG = 4
MESH = pl.DeviceIdType.MESH

CORE = ((0, 0),)
NEAR = ((-1, 0), (1, 0), (0, -1), (0, 1))
FAR = ((1, 1), (-1, -1), (1, -1), (-1, 1))
TURNS = (1, 2, 3, 0)
ISSUE = (2, 1, 3, 0)
CORE_ENTRIES = [(9 * a + 3 + c, 9 * d + 3 + c) for a, d in ((1, 1), (2, 0)) for c in range(3)]
NEAR_ENTRIES = [(9 * a + 3 * b + c, 9 * d + 3 * b + c) for a, d in ((1, 1), (2, 0)) for b in (0, 2) for c in range(3)]
NEAR_ENTRIES += [(3 + c, 21 + c) for c in range(3)]
FAR_ENTRIES = [(3 * b + c, 18 + 3 * b + c) for b in (0, 2) for c in range(3)]


def coefficients():
    center, spread = 1.0, 0.8
    sigma = center / spread
    rho = 1.0 / sigma
    old, new = [0.0], [1.0 / center]
    for _ in range(DEG - 1):
        following = 1.0 / (2.0 * sigma - rho)
        old.append(following * rho)
        new.append(2.0 * following / spread)
        rho = following
    return old, new


def kernel(sizes, blocks_hbm, order_hbm, pattern_hbm, start_hbm, rhs_hbm, out_ref,
           blocks, turned, order_ref, pattern, first, rhs, core, near, far, sent, tags, tag_out, core_table, near_table, masks, far_rows, spots, spot_of,
           load_sem, send_sem, core_sem, near_sem, far_sem, tag_send, tag_recv):
    nx, ny, nz = sizes
    gx, gy, gz = (lax.axis_index(a) for a in ("gx", "gy", "gz"))
    wide, _, depth, width = first.shape
    rows = wide * depth
    core_peers, near_peers, far_peers = 4 * len(CORE) - 1, 4 * len(NEAR), 4 * len(FAR)

    def at(dx, dy, dz):
        return (lax.rem(gx + (dx + nx), nx), lax.rem(gy + (dy + ny), ny), lax.rem(gz + dz, nz))

    barrier = pltpu.get_barrier_semaphore()
    for dz in ISSUE:
        for dx, dy in FAR + NEAR + CORE:
            if (dx, dy, dz) != (0, 0, 0):
                pl.semaphore_signal(barrier, inc=1, device_id=at(dx, dy, dz), device_id_type=MESH)

    small = [
        pltpu.make_async_copy(a, b, load_sem.at[1 + i])
        for i, (a, b) in enumerate(((order_hbm, order_ref), (start_hbm, first), (rhs_hbm, rhs), (pattern_hbm, pattern)))
    ]
    for copy in small:
        copy.start()
    load = pltpu.make_async_copy(blocks_hbm, blocks, load_sem.at[0])
    load.start()

    small[0].wait()
    lane = lax.broadcasted_iota(jnp.int32, (8, width), 1)
    own = lax.broadcasted_iota(jnp.int32, (8, width), 0)
    period = lane & (4 * rows - 1)
    row = period & (rows - 1)
    below = (gz + 3 - period // rows) & (nz - 1)
    place = (row // depth) * 8 + below * depth + (row & (depth - 1))
    tag = jnp.zeros((8, width), jnp.float32)
    for column in range(wide):
        for slot in range(8):
            value = order_ref[column, 0, slot].astype(jnp.float32)
            tag = jnp.where(place == column * 8 + slot, value, tag)
    tag_out[...] = tag

    for copy in small[1:]:
        copy.wait()
    filler = jnp.zeros((8 - rows, width), jnp.float32)
    v = jnp.concatenate([first[...].reshape(rows, width), filler], axis=0)
    remainder = jnp.concatenate([rhs[...].reshape(rows, width), filler], axis=0)
    sent[0] = v[0:rows].astype(jnp.bfloat16)

    def halo(groups):
        group = lane // (4 * rows)
        dx, dy = jnp.zeros_like(lane), jnp.zeros_like(lane)
        for g, (x, y) in enumerate(groups):
            dx = jnp.where(group == g, -x, dx)
            dy = jnp.where(group == g, -y, dy)
        inside = (gx + dx >= 0) & (gx + dx < nx) & (gy + dy >= 0) & (gy + dy < ny)
        inside = inside & (lane < 4 * rows * len(groups)) & (own < rows)
        step = wide * dx + (row // depth) - (own // depth)
        return jnp.where(inside & (step >= -1) & (step <= 1), (step + 1) * 3 + dy + 1, -1)

    mine = jnp.full((8, width), -100.0, jnp.float32)
    height = lax.broadcasted_iota(jnp.int32, (8, pattern.shape[-1]), 0)
    keep = jnp.zeros((8, pattern.shape[-1]), jnp.int32)
    for column in range(wide):
        present = pattern[column, 0]
        for slot in range(depth):
            r = column * depth + slot
            mine = jnp.where(own == r, order_ref[column, 0, gz * depth + slot].astype(jnp.float32), mine)
            line = jnp.sum(jnp.where(height == gz * depth + slot, present, 0), axis=0, keepdims=True)
            keep = jnp.where(height == r, line, keep)

    def premask(entries, groups, base):
        flat = halo(groups)
        for j, (low, high) in enumerate(entries):
            chosen = flat == jnp.where(own < depth, low // 3, high // 3)
            if low != 13:
                held = jnp.where(own[:, 0:1] < depth, keep[:, low : low + 1], keep[:, high : high + 1])
                chosen = chosen & (held > 0)
            masks[base + j] = jnp.where(chosen, 1.0, 0.0)

    premask(NEAR_ENTRIES, NEAR, 0)
    premask(FAR_ENTRIES, FAR, len(NEAR_ENTRIES))
    premask(CORE_ENTRIES, CORE, len(NEAR_ENTRIES + FAR_ENTRIES))

    pl.semaphore_wait(barrier, core_peers + near_peers + far_peers)

    def send(number):
        for groups, buffer, sem in ((FAR, far, far_sem), (NEAR, near, near_sem), (CORE, core, core_sem)):
            for dz in ISSUE:
                for g, (dx, dy) in enumerate(groups):
                    if (dx, dy, dz) == (0, 0, 0):
                        continue
                    slot = 4 * g + TURNS.index(dz)
                    pltpu.make_async_remote_copy(
                        sent.at[number], buffer.at[number, pl.ds(slot * rows, rows)], send_sem.at[number],
                        sem.at[number], device_id=at(dx, dy, dz), device_id_type=MESH,
                    ).start()

    everyone = FAR + NEAR + CORE
    for g, (dx, dy) in enumerate(everyone[:-1]):
        pltpu.make_async_remote_copy(
            tag_out, tags.at[g], tag_send, tag_recv, device_id=at(dx, dy, 0), device_id_type=MESH
        ).start()
    send(0)

    load.wait()
    unit = lax.broadcasted_iota(jnp.int32, (width, width), 0) == lax.broadcasted_iota(jnp.int32, (width, width), 1)
    unit = jnp.where(unit, 1.0, 0.0).astype(jnp.bfloat16)

    def turn_block(step, carry):
        for k in range(6):
            block = blocks[6 * step + k]
            flipped = block.T
            turned[6 * step + k] = flipped.astype(jnp.bfloat16)
        return carry

    lax.fori_loop(0, rows * 27 // 6, turn_block, 0)
    others = tags.at[pl.ds(0, len(everyone) - 1)]
    pltpu.make_async_copy(others, others, tag_recv).wait()
    tags[len(everyone) - 1] = tag

    def finish(entries, base, first_tag, count, table):
        plane = jnp.zeros((8, width), jnp.float32)
        for g in range(count):
            plane = jnp.where(lane // (4 * rows) == g, tags[first_tag + g], plane)
        level = [jnp.where(plane == mine + float(c - 1), 1.0, 0.0) for c in range(3)]
        parts = [masks[base + j] * level[low % 3] for j, (low, _) in enumerate(entries)]
        if len(parts) % 2:
            parts.append(jnp.zeros((8, width), jnp.float32))
        for j in range(0, len(parts), 2):
            both = jnp.concatenate(parts[j : j + 2], axis=0)
            table[pl.ds(8 * j, 16), :] = both.astype(jnp.bfloat16)

    finish(CORE_ENTRIES, len(NEAR_ENTRIES + FAR_ENTRIES), len(FAR + NEAR), len(CORE), core_table)
    finish(NEAR_ENTRIES, 0, len(FAR), len(NEAR), near_table)
    plane = jnp.zeros((8, width), jnp.float32)
    for g in range(len(FAR)):
        plane = jnp.where(lane // (4 * rows) == g, tags[g], plane)
    place = jnp.zeros((8, width), jnp.int32)
    for j, (low, _) in enumerate(FAR_ENTRIES):
        chosen = (masks[len(NEAR_ENTRIES) + j] > 0) & (plane == mine + float(low % 3 - 1))
        spot = jnp.max(jnp.where(chosen, (lane + 8).astype(jnp.float32), 0.0), axis=1, keepdims=True)
        place = jnp.where(lane == j, spot.astype(jnp.int32), place)
    spots[...] = place
    far_rows[pl.ds(0, 8), :] = jnp.zeros((8, width), jnp.float32)
    to_scalars = pltpu.make_async_copy(spots, spot_of, load_sem.at[1])
    to_scalars.start()

    old, new = coefficients()

    def weights(entries, r, first):
        pairs = entries[first : first + 2]
        blocks_of = [
            jnp.concatenate([turned[(r + s) * 27 + pair[r // depth]] for s in range(depth)], axis=1) for pair in pairs
        ]
        if len(pairs) == 1:
            blocks_of.append(jnp.zeros((width, 2 * width), jnp.bfloat16))
        return jnp.concatenate(blocks_of, axis=0)

    def own_rows(totals):
        product = jnp.zeros((8, width), jnp.float32)
        for total, r in zip(totals, range(0, rows, depth)):
            for s in range(depth):
                product = jnp.where(own == r + s, total[:, s * width : (s + 1) * width], product)
        return product

    def nearby(entries, table_ref, theirs, sem, group, picked_0, unit_0, unit_1):
        units = list(zip((unit_0, unit_1), range(0, rows, depth)))
        pltpu.matmul_push_rhs(weights(entries, units[1][1], 0), 0, 1)
        pltpu.matmul_push_rhs(weights(entries, units[1][1], 2), 1, 1)
        pltpu.matmul_push_rhs(weights(entries, units[0][1], 0), 1, 0)
        pltpu.make_async_copy(theirs, theirs, sem).wait()
        seen = group[...]
        seen = jnp.concatenate([seen, jnp.zeros((2 * width - seen.shape[0], width), jnp.bfloat16)], axis=0)
        pltpu.matmul_push_rhs(jnp.concatenate([seen, jnp.zeros_like(seen)], axis=1), 0, 0)
        table = table_ref[...]
        pltpu.matmul_acc_lhs(picked_0, jnp.concatenate([table, jnp.zeros_like(table)], axis=1), 0)
        pltpu.matmul_push_rhs(weights(entries, units[0][1], 2), 0, 0)
        picked = pltpu.matmul_pop(picked_0)[:, 0:width]
        for n, first in enumerate(range(0, len(entries), 2)):
            left = jnp.concatenate([picked[8 * first : 8 * first + 8], picked[8 * first + 8 : 8 * first + 16]], axis=1)
            left = jnp.concatenate([left, jnp.zeros_like(left)], axis=0).astype(jnp.bfloat16)
            for i, (acc, r) in enumerate(units):
                staged = (n + 1 - i) % 2
                pltpu.matmul_acc_lhs(acc, left, staged)
                if first + 4 < len(entries):
                    pltpu.matmul_push_rhs(weights(entries, r, first + 4), staged, i)
        return own_rows([pltpu.matmul_pop(acc)[0:8] for acc, _ in units])

    def diagonal_row(spots_now, r, j):
        part = jnp.broadcast_to(far_rows[pl.ds(spots_now[r][j], 1), :], (8, width))
        for s in range(1, depth):
            line = jnp.broadcast_to(far_rows[pl.ds(spots_now[r + s][j], 1), :], (8, width))
            part = jnp.where(own == r + s, line, part)
        return part

    def diagonal_left(spots_now, r, first):
        left = jnp.concatenate([diagonal_row(spots_now, r, first), diagonal_row(spots_now, r, first + 1)], axis=1)
        return jnp.concatenate([left, jnp.zeros_like(left)], axis=0).astype(jnp.bfloat16)

    def diagonal(number, unit_0, unit_1):
        units = list(zip((unit_0, unit_1), range(0, rows, depth)))
        for i, (acc, r) in enumerate(units):
            pltpu.matmul_push_rhs(weights(FAR_ENTRIES, r, 0), 0, i)
            pltpu.matmul_acc_lhs(acc, jnp.zeros((16, 2 * width), jnp.bfloat16), 0)
            pltpu.matmul_push_rhs(weights(FAR_ENTRIES, r, 2), 0, i)
            pltpu.matmul_push_rhs(weights(FAR_ENTRIES, r, 4), 1, i)
        last = far_rows.shape[0] - 1
        spots_now = [[jnp.clip(spot_of[r, j], 0, last) for j in range(len(FAR_ENTRIES))] for r in range(rows)]
        theirs = far.at[number]
        pltpu.make_async_copy(theirs, theirs, far_sem.at[number]).wait()
        far_rows[pl.ds(8, 4 * rows * len(FAR)), :] = far[number].astype(jnp.float32)
        for first, staged in ((0, None), (2, 0), (4, 1)):
            for acc, r in units:
                pltpu.matmul_acc_lhs(acc, diagonal_left(spots_now, r, first), staged)
        return own_rows([pltpu.matmul_pop(acc)[0:8] for acc, _ in units])

    def turn_of(number, carry):
        v, smoothed, remainder = carry
        a, b = jnp.float32(old[0]), jnp.float32(new[0])
        for i in range(1, DEG):
            a = jnp.where(number == i, jnp.float32(old[i]), a)
            b = jnp.where(number == i, jnp.float32(new[i]), b)
        core[number, pl.ds(core_peers * rows, rows)] = sent[number]
        def applied(entries, table, theirs, sem, group):
            return pl.run_scoped(
                functools.partial(nearby, entries, table, theirs, sem, group),
                pltpu.ACC(0)((table.shape[0], 2 * width), jnp.float32),
                pltpu.ACC(0)((16, 2 * width), jnp.float32),
                pltpu.ACC(1)((16, 2 * width), jnp.float32),
            )

        mates = core.at[number, pl.ds(0, core_peers * rows)]
        partial = remainder - applied(CORE_ENTRIES, core_table, mates, core_sem.at[number], core.at[number])
        partial = partial - applied(NEAR_ENTRIES, near_table, near.at[number], near_sem.at[number], near.at[number])
        remainder = partial - pl.run_scoped(
            functools.partial(diagonal, number),
            pltpu.ACC(0)((16, 2 * width), jnp.float32),
            pltpu.ACC(1)((16, 2 * width), jnp.float32),
        )
        following = a * v + b * remainder

        @pl.when(number < DEG)
        def _():
            sent[number + 1] = following[0:rows].astype(jnp.bfloat16)
            send(number + 1)

        return following, smoothed + v, remainder

    to_scalars.wait()
    _, smoothed, remainder = lax.fori_loop(0, DEG + 1, turn_of, (v, jnp.zeros_like(v), remainder))
    out_ref[0] = smoothed[0:rows].reshape(first.shape)
    out_ref[1] = remainder[0:rows].reshape(first.shape)

    pltpu.make_async_copy(others, others, tag_send).wait()

    def drain(number, carry):
        for theirs in (core.at[number, pl.ds(0, core_peers * rows)], near.at[number], far.at[number]):
            pltpu.make_async_copy(theirs, theirs, send_sem.at[number]).wait()
        return carry

    lax.fori_loop(0, DEG + 1, drain, 0)


def split(both_ref, smoothed_hbm, remainder_hbm, sem):
    copies = [
        pltpu.make_async_copy(both_ref.at[i], out, sem.at[i]) for i, out in enumerate((smoothed_hbm, remainder_hbm))
    ]
    for copy in copies:
        copy.start()
    for copy in copies:
        copy.wait()


def local(sizes, blocks, pattern, order, start, rhs):
    wide, _, depth, width = start.shape
    rows = wide * depth
    flat = blocks.reshape((rows * blocks.shape[3],) + blocks.shape[4:])
    vmem = pl.BlockSpec(memory_space=pltpu.VMEM)
    anywhere = pl.BlockSpec(memory_space=pl.ANY)
    core_blocks, near_blocks = (len(CORE_ENTRIES) + 1) // 2, (len(NEAR_ENTRIES) + 1) // 2
    both = pl.pallas_call(
        functools.partial(kernel, sizes),
        out_shape=pltpu.VMEM((2,) + start.shape, jnp.float32),
        in_specs=[anywhere, anywhere, anywhere, anywhere, anywhere],
        out_specs=vmem,
        scratch_shapes=[
            pltpu.VMEM(flat.shape, jnp.bfloat16),
            pltpu.VMEM(flat.shape, jnp.bfloat16),
            pltpu.SMEM(order.shape, jnp.int32),
            pltpu.VMEM(pattern.shape, jnp.int32),
            pltpu.VMEM(start.shape, jnp.float32),
            pltpu.VMEM(start.shape, jnp.float32),
            pltpu.VMEM((DEG + 1, 4 * rows * len(CORE), width), jnp.bfloat16),
            pltpu.VMEM((DEG + 1, 4 * rows * len(NEAR), width), jnp.bfloat16),
            pltpu.VMEM((DEG + 1, 4 * rows * len(FAR), width), jnp.bfloat16),
            pltpu.VMEM((DEG + 1, rows, width), jnp.bfloat16),
            pltpu.VMEM((len(CORE + NEAR + FAR), 8, width), jnp.float32),
            pltpu.VMEM((8, width), jnp.float32),
            pltpu.VMEM((16 * core_blocks, width), jnp.bfloat16),
            pltpu.VMEM((16 * near_blocks, width), jnp.bfloat16),
            pltpu.VMEM((len(NEAR_ENTRIES + FAR_ENTRIES + CORE_ENTRIES), 8, width), jnp.float32),
            pltpu.VMEM((8 + 4 * rows * len(FAR), width), jnp.float32),
            pltpu.VMEM((8, width), jnp.int32),
            pltpu.SMEM((8, width), jnp.int32),
            pltpu.SemaphoreType.DMA((5,)),
            pltpu.SemaphoreType.DMA((DEG + 1,)),
            pltpu.SemaphoreType.DMA((DEG + 1,)),
            pltpu.SemaphoreType.DMA((DEG + 1,)),
            pltpu.SemaphoreType.DMA((DEG + 1,)),
            pltpu.SemaphoreType.DMA,
            pltpu.SemaphoreType.DMA,
        ],
        compiler_params=pltpu.CompilerParams(collective_id=0, has_side_effects=True),
    )(flat, order, pattern, start, rhs)
    both = pltpu.with_memory_space_constraint(both, pltpu.VMEM)
    piece = jax.ShapeDtypeStruct(start.shape, jnp.float32)
    return pl.pallas_call(
        split,
        out_shape=(piece, piece),
        in_specs=[vmem],
        out_specs=(anywhere, anywhere),
        scratch_shapes=[pltpu.SemaphoreType.DMA((2,))],
    )(both)


def solution(mesh):
    in_specs = (
        P("gx", "gy", "gz", None, None, None),
        P("gx", "gy", None, None),
        P("gx", "gy", None),
        P("gx", "gy", "gz", None),
        P("gx", "gy", "gz", None),
    )
    out_specs = (P("gx", "gy", "gz", None), P("gx", "gy", "gz", None))
    sizes = tuple(mesh.shape[a] for a in ("gx", "gy", "gz"))
    return jax.shard_map(
        functools.partial(local, sizes), mesh=mesh, in_specs=in_specs, out_specs=out_specs, check_vma=False
    )
```
